32 devices in a mesh: batch: 8 (over y, x, core), pos: 4 (over z).
Axes of the slice: x: 2, y: 2, z: 4, core: 2. Of those that a mesh axis runs over, the one named last changes fastest.
Arguments:
- tokens: bfloat16 [64, 512, 512], P('batch', 'pos'), may hold values from -6 to 6
- cotangent: bfloat16 [64, 512, 512], P('batch', 'pos'), may hold values from -6 to 6
- segment_ids: int32 [64, 512], P('batch'), may hold values from 0 to 5, never falling along the last dimension, each value on 1 to 256 neighbouring positions
- pad_mask: int32 [64, 512], P('batch'), may hold values 0 or 1
- skip_flags: int32 [64], P('batch'), may hold values from 0 to 1, as said below
- in_master: float32 [1572864], P(('batch', 'pos')), may hold values from -0.25 to 0.25
- spatial_master: float32 [262144], P(('batch', 'pos')), may hold values from -0.5 to 0.5
- out_master: float32 [786432], P(('batch', 'pos')), may hold values from -0.15625 to 0.15625
- vector_master: float32 [8192], P(('batch', 'pos')), may hold values from -0.5 to 1.5, as said below
- in_first: float32 [1572864], P(('batch', 'pos')), may hold values from -48 to 48
- spatial_first: float32 [262144], P(('batch', 'pos')), may hold values from -40 to 40
- out_first: float32 [786432], P(('batch', 'pos')), may hold values from -128 to 128
- vector_first: float32 [8192], P(('batch', 'pos')), may hold values from -40.22652 to 40.22652
- in_second: float32 [1572864], P(('batch', 'pos')), may hold values from 5.24288 to 20.97152
- spatial_second: float32 [262144], P(('batch', 'pos')), may hold values from 3.93216 to 15.72864
- out_second: float32 [786432], P(('batch', 'pos')), may hold values from 32.768 to 131.072
- vector_second: float32 [8192], P(('batch', 'pos')), may hold values from 3.5684352 to 131.072, as said below
Outputs:
- mixed: bfloat16 [64, 512, 512], P('batch', 'pos')
- input_grad: float32 [64, 512, 512], P('batch', 'pos')
- in_master_new: float32 [1572864], P(('batch', 'pos'))
- in_first_new: float32 [1572864], P(('batch', 'pos'))
- in_second_new: float32 [1572864], P(('batch', 'pos'))
- spatial_master_new: float32 [262144], P(('batch', 'pos'))
- spatial_first_new: float32 [262144], P(('batch', 'pos'))
- spatial_second_new: float32 [262144], P(('batch', 'pos'))
- out_master_new: float32 [786432], P(('batch', 'pos'))
- out_first_new: float32 [786432], P(('batch', 'pos'))
- out_second_new: float32 [786432], P(('batch', 'pos'))
- vector_master_new: float32 [8192], P(('batch', 'pos'))
- vector_first_new: float32 [8192], P(('batch', 'pos'))
- vector_second_new: float32 [8192], P(('batch', 'pos'))
The draws below stay inside these ranges and needn't reach their ends.
Inputs may be any that keep to these rules, and one draw needn't show every extreme that they name: `vector_master`: gains lie in 0.6 to 1.4, the spatial bias in 0.5 to 1.5, the other biases in -0.5 to 0.5. `vector_second`: all entries are positive. `skip_flags`: values are 0 or 1; at least one row skips.
All inputs are finite; a program needn't handle non-finite values. No bound on the sum of `pad_mask` on one device may be relied on, other than what follows from the above.
Results may differ from the reference program's by a relative error of at most 0.011.
Values may be sent and summed in bfloat16 or wider, within the bound.
No kernel may reach another device: no remote copies, remote signals or barrier semaphores. Data moves between devices by JAX's collectives and lax.ppermute only.
A program may use at most 192 MiB of HBM per device.

```python
import math
import jax
import jax.numpy as jnp
import numpy as np
from jax import lax

D = 512
HID = 3072
SEQ = 512
ROWS_DEV = 8
GATE = 1536
ROWS = 64
TOKENS = 32768
VEC = 8192


def vector_scales():
    tokens_root = jnp.sqrt(jnp.float32(TOKENS))
    spatial_root = jnp.sqrt(jnp.float32(ROWS * GATE))
    return jnp.concatenate([jnp.ones((D,), jnp.float32) * tokens_root, jnp.ones((D,), jnp.float32) * tokens_root, jnp.ones((HID,), jnp.float32) * (0.4 * tokens_root), jnp.ones((GATE,), jnp.float32) * (0.33 * tokens_root), jnp.ones((GATE,), jnp.float32) * (0.33 * tokens_root), jnp.ones((SEQ,), jnp.float32) * (0.4 * spatial_root), jnp.ones((D,), jnp.float32) * (0.9 * tokens_root)])


def draw_skip_flags(key, part):
    first_key, second_key = jax.random.split(jax.random.fold_in(key, 21), 2)
    forced = jax.random.randint(first_key, (), 0, ROWS)
    chance = jax.random.randint(second_key, (ROWS,), 0, 100)
    places = jnp.arange(ROWS, dtype=jnp.int32)
    return jnp.where((chance < 8) | (places == forced), 1, 0).astype(jnp.int32)


def draw_vector_master(key, part):
    first_key, second_key, third_key = jax.random.split(jax.random.fold_in(key, 11), 3)
    gain_like = jax.random.uniform(first_key, (VEC,), jnp.float32, 0.6, 1.4)
    bias_like = jax.random.uniform(second_key, (VEC,), jnp.float32, -0.5, 0.5)
    spatial_like = jax.random.uniform(third_key, (VEC,), jnp.float32, 0.5, 1.5)
    kind_codes = jnp.concatenate([jnp.zeros((D,), jnp.int32), jnp.ones((D,), jnp.int32), jnp.ones((HID,), jnp.int32), jnp.zeros((GATE,), jnp.int32), jnp.ones((GATE,), jnp.int32), jnp.full((SEQ,), 2, jnp.int32), jnp.ones((D,), jnp.int32)])
    return jnp.where(kind_codes == 0, gain_like, jnp.where(kind_codes == 1, bias_like, spatial_like))


def draw_vector_first(key, part):
    values = jax.random.uniform(jax.random.fold_in(key, 12), (VEC,), jnp.float32, -2.0, 2.0)
    return values * vector_scales() / 9.0


def draw_vector_second(key, part):
    factor = jnp.exp(jax.random.uniform(jax.random.fold_in(key, 13), (VEC,), jnp.float32, 0.0, jnp.log(4.0)))
    scales = vector_scales()
    return factor * 0.001 * scales * scales


def place_ends(values, key, least, largest):
    longest = values.shape.index(max(values.shape))
    spots = []
    for shift in (0, 1):
        where = [jax.random.randint(jax.random.fold_in(key, axis), (), 0, length) for axis, length in enumerate(values.shape)]
        where[longest] = (where[longest] + shift) % values.shape[longest]
        spots.append(tuple(where))
    return values.at[spots[0]].set(least).at[spots[1]].set(largest)


def levels(rng, shape, shards, low, top_value):
    loudness, own = 1.0, jax.random.fold_in(rng, 6)
    for axis_at, blocks in shards:
        heights = jnp.exp(jax.random.uniform(jax.random.fold_in(own, axis_at), (blocks,), jnp.float32, low / len(shards), top_value / len(shards)))
        loudness = loudness * jnp.repeat(heights, shape[axis_at] // blocks).reshape([-1 if axis == axis_at else 1 for axis in range(len(shape))])
    return loudness


def profile(amount, total, bound, slope):
    weights = [(1 << 20) // math.isqrt(rank ** slope) + 1 for rank in range(2, amount + 1)]
    surplus, holding = total - bound - (amount - 1), [1] * (amount - 1)
    while surplus > 0:
        free = [i for i in range(amount - 1) if holding[i] < bound]
        whole, left = sum([weights[i] for i in free]), surplus
        for i in free:
            extra = min(bound - holding[i], max(1, left * weights[i] // whole), surplus)
            holding[i] = holding[i] + extra
            surplus = surplus - extra
    return np.array([bound] + holding)


def uneven_parts(key, amount, total, limit, skew):
    if amount == 2:
        one = jax.random.randint(key, (), max(1, total - limit), min(limit, total - 1) + 1)
        return jnp.stack([one, total - one])
    tallies = jnp.asarray(profile(amount, total, limit, skew), jnp.int32)
    pairs = (amount - 1) // 2
    source_of, sink = tallies[1:1 + 2 * pairs:2], tallies[2:2 + 2 * pairs:2]
    room = jnp.minimum(source_of - 1, limit - sink)
    passed = jax.random.randint(jax.random.fold_in(key, 1), (pairs,), 0, 1 << 20) % (room + 1)
    tallies = tallies.at[1:1 + 2 * pairs:2].set(source_of - passed).at[2:2 + 2 * pairs:2].set(sink + passed)
    return tallies[jax.random.permutation(jax.random.fold_in(key, 2), amount)]


def gaussian(key, extent, width, most, shards=(), kind=jnp.bfloat16):
    values = width * jax.random.normal(key, extent, jnp.float32)
    if shards:
        values = values * levels(key, extent, shards, -0.22, 0.18)
    return jnp.clip(values, -most, most).astype(kind)


def setup_inputs(seed: int = 0) -> dict:
    arg_keys = jax.random.split(jax.random.key(seed), 18)
    tokens = gaussian(arg_keys[0], (ROWS, SEQ, D), 1.0, 6.0, ((0, 8), (1, 4)))
    cotangent = gaussian(arg_keys[1], (ROWS, SEQ, D), 1.0, 6.0, ((0, 8), (1, 4)))
    segment_ids = jax.vmap(lambda own: jnp.searchsorted(jnp.cumsum(uneven_parts(own, 6, SEQ, SEQ // 2, 1)), jnp.arange(SEQ), side="right"))(jax.random.split(arg_keys[2], ROWS)).reshape((ROWS, SEQ)).astype(jnp.int32)
    pad_mask = place_ends((jax.random.randint(arg_keys[3], (ROWS, SEQ), 0, 16) < 15).astype(jnp.int32), jax.random.fold_in(arg_keys[3], 1), 0, 1)
    skip_flags = draw_skip_flags(jax.random.fold_in(arg_keys[17], 71), 0)
    in_master = gaussian(arg_keys[5], (D * HID,), D ** -0.5, 0.25, ((0, 32),), jnp.float32)
    spatial_master = gaussian(arg_keys[6], (SEQ * SEQ,), (SEQ // 4) ** -0.5, 0.5, ((0, 32),), jnp.float32)
    out_master = gaussian(arg_keys[7], (GATE * D,), GATE ** -0.5, 0.15625, ((0, 32),), jnp.float32)
    vector_master = draw_vector_master(jax.random.fold_in(arg_keys[17], 71), 0)
    in_first = gaussian(arg_keys[9], (D * HID,), (0.4 * TOKENS ** 0.5 / 9), 48.0, ((0, 32),), jnp.float32)
    spatial_first = gaussian(arg_keys[10], (SEQ * SEQ,), (0.2 * (ROWS * GATE) ** 0.5 / 9), 40.0, ((0, 32),), jnp.float32)
    out_first = gaussian(arg_keys[11], (GATE * D,), (TOKENS ** 0.5 / 9), 128.0, ((0, 32),), jnp.float32)
    vector_first = draw_vector_first(jax.random.fold_in(arg_keys[17], 71), 0)
    in_second = jnp.clip(jnp.exp(math.log(20.97152) - 1.3862944 * jax.random.uniform(arg_keys[13], (D * HID,), jnp.float32) ** levels(arg_keys[13], (D * HID,), ((0, 32),), -0.2, 0.2)), 5.24288, 20.97152)
    spatial_second = jnp.clip(jnp.exp(math.log(15.72864) - 1.3862944 * jax.random.uniform(arg_keys[14], (SEQ * SEQ,), jnp.float32) ** levels(arg_keys[14], (SEQ * SEQ,), ((0, 32),), -0.2, 0.2)), 3.93216, 15.72864)
    out_second = jnp.clip(jnp.exp(math.log(131.072) - 1.3862944 * jax.random.uniform(arg_keys[15], (GATE * D,), jnp.float32) ** levels(arg_keys[15], (GATE * D,), ((0, 32),), -0.2, 0.2)), 32.768, 131.072)
    vector_second = draw_vector_second(jax.random.fold_in(arg_keys[17], 71), 0)
    return {"tokens": tokens, "cotangent": cotangent, "segment_ids": segment_ids, "pad_mask": pad_mask, "skip_flags": skip_flags, "in_master": in_master, "spatial_master": spatial_master, "out_master": out_master, "vector_master": vector_master, "in_first": in_first, "spatial_first": spatial_first, "out_first": out_first, "vector_first": vector_first, "in_second": in_second, "spatial_second": spatial_second, "out_second": out_second, "vector_second": vector_second}


norm_eps = 1e-05
beta_one = 0.9
beta_two = 0.999
adam_eps = 1e-08
step_count = 10.0
decay_matrix = 0.1
rate_in = 0.12
rate_spatial = 0.2
rate_out = 0.07
rate_vector = 1.0

@jax.custom_vjp
def low(v):
    return lax.optimization_barrier(v.astype(jnp.bfloat16)).astype(jnp.float32)

@jax.custom_vjp
def low_back(v):
    return v

def low_keep(v):
    return (low(v), None)

def low_pass(kept, grad):
    return (grad,)

def back_keep(v):
    return (v, None)

def back_low(kept, grad):
    return (low(grad),)
low.defvjp(low_keep, low_pass)
low_back.defvjp(back_keep, back_low)

def split_vector(vector):
    lengths = [D, D, HID, GATE, GATE, SEQ, D]
    pieces = []
    cursor = 0
    for length in lengths:
        pieces.append(vector[cursor:cursor + length])
        cursor = cursor + length
    return pieces

def layer_norm(values):
    average = lax.optimization_barrier(jnp.mean(values, -1, keepdims=True))
    centred = values - average
    spread = lax.optimization_barrier(jnp.mean(centred * centred, -1, keepdims=True))
    return centred * lax.rsqrt(spread + norm_eps)

def forward(masters, inputs, segments, padding, keeping):
    in_master, spatial_master, out_master, vector_master = masters
    highest = lax.Precision.HIGHEST
    weight_in = low(in_master).reshape(D, HID)
    weight_spatial = low(spatial_master).reshape(SEQ, SEQ)
    weight_out = low(out_master).reshape(GATE, D)
    gain_in, bias_in, bias_hidden, gain_gate, bias_gate, bias_spatial, bias_out = split_vector(low(vector_master))
    scaled_in = low(layer_norm(inputs) * gain_in + bias_in)
    hidden_pre = low_back(jnp.einsum('bsd,dh->bsh', scaled_in, weight_in, precision=highest)) + bias_hidden
    hidden = jax.nn.gelu(hidden_pre, approximate=False)
    left_half = hidden[..., :GATE]
    gate_low = low(layer_norm(hidden[..., GATE:]) * gain_gate + bias_gate)
    same_seg = (segments[:, :, None] == segments[:, None, :]) & (padding[:, None, :] == 1)
    mixing = jnp.where(same_seg, weight_spatial[None], 0.0)
    spatial = low_back(jnp.einsum('bij,bjc->bic', mixing, gate_low, precision=highest)) + bias_spatial[None, :, None]
    gated = low(left_half * spatial)
    branch = jnp.einsum('bsg,gd->bsd', gated, weight_out, precision=highest) + bias_out
    return inputs + branch * keeping[..., None]

def adamw(master, first, second, gradient, rate, decay):
    first_new = beta_one * first + (1.0 - beta_one) * gradient
    second_new = beta_two * second + (1.0 - beta_two) * gradient * gradient
    first_hat = first_new / (1.0 - beta_one ** step_count)
    second_hat = second_new / (1.0 - beta_two ** step_count)
    master_new = master - rate * (first_hat / (jnp.sqrt(second_hat) + adam_eps) + decay * master)
    return (master_new, first_new, second_new)

def reference(tokens, cotangent, segment_ids, pad_mask, skip_flags, in_master, spatial_master, out_master, vector_master, in_first, spatial_first, out_first, vector_first, in_second, spatial_second, out_second, vector_second):
    masters = (in_master, spatial_master, out_master, vector_master)
    keeping = pad_mask.astype(jnp.float32) * (1.0 - skip_flags.astype(jnp.float32))[:, None]
    block_total = ROWS // ROWS_DEV

    def blocked(array):
        return array.reshape((block_total, ROWS_DEV) + array.shape[1:])

    def one_block(totals, block_item):
        inputs, back_block, segments, padding, keep_block = block_item

        def local_forward(params, values):
            return forward(params, values, segments, padding, keep_block)
        output, pullback = jax.vjp(local_forward, masters, inputs.astype(jnp.float32))
        grad_params, grad_inputs = pullback(back_block.astype(jnp.float32))
        totals = tuple((total_part + grad_part for total_part, grad_part in zip(totals, grad_params)))
        return (totals, (output.astype(jnp.bfloat16), grad_inputs))
    initial = tuple((jnp.zeros_like(master_flat) for master_flat in masters))
    grads, outputs = lax.scan(one_block, initial, (blocked(tokens), blocked(cotangent), blocked(segment_ids), blocked(pad_mask), blocked(keeping)))
    mixed = outputs[0].reshape(ROWS, SEQ, D)
    input_grad = outputs[1].reshape(ROWS, SEQ, D)
    in_new = adamw(in_master, in_first, in_second, grads[0], rate_in, decay_matrix)
    spatial_new = adamw(spatial_master, spatial_first, spatial_second, grads[1], rate_spatial, decay_matrix)
    out_new = adamw(out_master, out_first, out_second, grads[2], rate_out, decay_matrix)
    vector_new = adamw(vector_master, vector_first, vector_second, grads[3], rate_vector, 0.0)
    return (mixed, input_grad, in_new[0], in_new[1], in_new[2], spatial_new[0], spatial_new[1], spatial_new[2], out_new[0], out_new[1], out_new[2], vector_new[0], vector_new[1], vector_new[2])
```

```python
import jax
import jax.numpy as jnp
from jax import lax
from jax.sharding import PartitionSpec as P

D = 512
HID = 3072
SEQ = 512
GATE = 1536
LANE = 128

norm_eps = 1e-05
beta_one = 0.9
beta_two = 0.999
adam_eps = 1e-08
step_count = 10.0
decay_matrix = 0.1
rate_in = 0.12
rate_spatial = 0.2
rate_out = 0.07
rate_vector = 1.0

low_type = jnp.bfloat16
wide = jnp.float32


def split_vector(vector):
    lengths = [D, D, HID, GATE, GATE, SEQ, D]
    pieces = []
    cursor = 0
    for length in lengths:
        pieces.append(vector[cursor : cursor + length])
        cursor = cursor + length
    return pieces


def norm_parts(values):
    average = jnp.mean(values, -1, keepdims=True)
    centred = values - average
    spread = jnp.mean(centred * centred, -1, keepdims=True)
    inverse = lax.rsqrt(spread + norm_eps)
    return (centred * inverse, inverse)


def norm_back(grad_hat, normed, inverse):
    first_mean = jnp.mean(grad_hat, -1, keepdims=True)
    cross_mean = jnp.mean(grad_hat * normed, -1, keepdims=True)
    return (grad_hat - first_mean - normed * cross_mean) * inverse


def gelu_exact(values):
    return jax.nn.gelu(values, approximate=False)


def adamw(master, first, second, gradient, rate, decay):
    first_new = beta_one * first + (1.0 - beta_one) * gradient
    second_new = beta_two * second + (1.0 - beta_two) * gradient * gradient
    first_hat = first_new / (1.0 - beta_one**step_count)
    second_hat = second_new / (1.0 - beta_two**step_count)
    master_new = master - rate * (first_hat / (jnp.sqrt(second_hat) + adam_eps) + decay * master)
    return (master_new, first_new, second_new)


def swap(value, axis, size, mask):
    return lax.ppermute(value, axis, [(i, i ^ mask) for i in range(size)])


def bit_count(size):
    bits = size.bit_length() - 1
    assert size == 1 << bits
    return bits


def batch_rounds(bits):
    if bits == 3:
        return [(1, 2), (0,)]
    return [(b,) for b in range(1, bits)] + [(0,)]


def gather_blocks(block, sizes, place):
    batch_size, pos_size = sizes
    b, z = place
    rows, cols = block.shape
    bits = bit_count(batch_size)
    zbits = bit_count(pos_size)
    total = bits + zbits
    held = block.reshape((1,) * total + (rows, cols))

    def exchange(held, axis_name, size, index, group, shift):
        pieces = [held]
        for g in range(1, 1 << len(group)):
            mask = sum((1 << group[i]) for i in range(len(group)) if (g >> i) & 1)
            pieces.append(swap(held, axis_name, size, mask))
        for bit in group:
            axis = total - 1 - (bit + shift)
            mine = (index >> bit) & 1
            merged = []
            for a, c in zip(pieces[0::2], pieces[1::2]):
                merged.append(
                    jnp.where(
                        mine == 0,
                        jnp.concatenate([a, c], axis),
                        jnp.concatenate([c, a], axis),
                    )
                )
            pieces = merged
        return pieces[0]

    for bit in reversed(range(zbits)):
        held = exchange(held, "pos", pos_size, z, (bit,), 0)
    for group in batch_rounds(bits):
        held = exchange(held, "batch", batch_size, b, group, zbits)
    return held.reshape(batch_size * pos_size * rows, cols)


def reduce_blocks(grad, sizes, place):
    batch_size, pos_size = sizes
    b, z = place
    bits = bit_count(batch_size)
    zbits = bit_count(pos_size)
    total = bits + zbits
    cols = grad.shape[1]
    rows = grad.shape[0] // (batch_size * pos_size)
    held = grad.reshape((2,) * total + (rows, cols))

    def halve(held, axis_name, size, index, group, shift):
        parts = {0: held}
        for i, bit in enumerate(group):
            axis = total - 1 - (bit + shift)
            mine = (index >> bit) & 1
            spread = {}
            for g, part in parts.items():
                spread[g] = lax.dynamic_slice_in_dim(part, mine, 1, axis)
                spread[g | (1 << i)] = lax.dynamic_slice_in_dim(part, 1 - mine, 1, axis)
            parts = spread
        summed = parts[0].astype(wide)
        for g, part in parts.items():
            if g:
                mask = sum((1 << group[i]) for i in range(len(group)) if (g >> i) & 1)
                summed = summed + swap(part, axis_name, size, mask).astype(wide)
        return summed.astype(grad.dtype)

    for group in reversed(batch_rounds(bits)):
        held = halve(held, "batch", batch_size, b, group, zbits)
    for bit in range(zbits):
        held = halve(held, "pos", pos_size, z, (bit,), 0)
    return held.reshape(rows, cols)


def local_fn(sizes):
    batch_size, pos_size = sizes

    def local(
        tokens,
        cotangent,
        segment_ids,
        pad_mask,
        skip_flags,
        in_master,
        spatial_master,
        out_master,
        vector_master,
        in_first,
        spatial_first,
        out_first,
        vector_first,
        in_second,
        spatial_second,
        out_second,
        vector_second,
    ):
        b = lax.axis_index("batch")
        z = lax.axis_index("pos")
        place = (b, z)
        devices = batch_size * pos_size
        rows = tokens.shape[0]
        length = tokens.shape[1]
        mine = rows // pos_size

        def relative(value, axis):
            return jnp.concatenate(
                [
                    lax.dynamic_slice_in_dim(
                        value, (z ^ k) * (value.shape[axis] // pos_size), value.shape[axis] // pos_size, axis
                    )
                    for k in range(pos_size)
                ],
                axis,
            )

        def to_rows(value):
            parts = []
            for k in range(pos_size):
                part = lax.dynamic_slice_in_dim(value, (z ^ k) * mine, mine, 0)
                parts.append(part if k == 0 else swap(part, "pos", pos_size, k))
            return jnp.concatenate(parts, 1)

        def to_places(value):
            parts = []
            for k in range(pos_size):
                part = lax.slice_in_dim(value, k * length, (k + 1) * length, axis=1)
                parts.append(part if k == 0 else swap(part, "pos", pos_size, k))
            return relative(jnp.concatenate(parts, 0), 0)

        in_rows = D // devices if D % devices == 0 else 1
        in_block = in_master.astype(low_type).reshape(in_rows, -1)
        vector_block = vector_master.astype(low_type).reshape(in_rows, -1)
        vector_cols = vector_block.shape[1]
        vector_block = jnp.pad(vector_block, ((0, 0), (0, LANE - vector_cols)))
        in_block = jnp.concatenate([in_block, vector_block], 1)
        spatial_block = spatial_master.astype(low_type).reshape(-1, D)
        out_block = out_master.astype(low_type).reshape(-1, D)
        rest_block = jnp.concatenate([spatial_block, out_block], 0)
        spatial_rows = spatial_block.shape[0]
        in_width = in_master.shape[0] // in_rows

        in_all = gather_blocks(in_block, sizes, place)
        inputs_low = to_rows(tokens)
        rest_all = gather_blocks(rest_block, sizes, place).reshape(devices, -1, D)
        back_low = to_rows(cotangent)

        weight_in = in_all[:, :in_width].reshape(D, HID)
        vector_flat = in_all[:, in_width : in_width + vector_cols].reshape(-1)
        weight_spatial = rest_all[:, :spatial_rows].reshape(SEQ, SEQ)
        weight_out = rest_all[:, spatial_rows:].reshape(GATE, D)
        gain_in, bias_in, bias_hidden, gain_gate, bias_gate, bias_spatial, bias_out = split_vector(
            vector_flat.astype(wide)
        )

        own_rows = lambda value: lax.dynamic_slice_in_dim(value, z * mine, mine, 0)
        segments = relative(own_rows(segment_ids), 1)
        padding = relative(own_rows(pad_mask), 1)
        keeping = padding.astype(wide) * (1.0 - own_rows(skip_flags).astype(wide))[:, None]
        keep_flat = keeping.reshape(-1, 1)
        same_rows = (segments[:, :, None] == segments[:, None, :]) & (padding[:, None, :] == 1)
        mixing_rows = relative(relative(weight_spatial, 0), 1)
        bias_rows = relative(bias_spatial, 0)
        mixing = jnp.where(same_rows, mixing_rows[None], jnp.zeros((), low_type))

        inputs = inputs_low.astype(wide).reshape(-1, D)
        normed_in, inverse_in = norm_parts(inputs)
        scaled_in = (normed_in * gain_in + bias_in).astype(low_type)
        hidden_pre = jnp.dot(scaled_in, weight_in, preferred_element_type=wide) + bias_hidden
        hidden, gelu_back = jax.vjp(gelu_exact, hidden_pre)
        left_half = hidden[:, :GATE]
        normed_gate, inverse_gate = norm_parts(hidden[:, GATE:])
        gate_low = (normed_gate * gain_gate + bias_gate).astype(low_type).reshape(mine, SEQ, GATE)
        spatial = (
            jnp.einsum("rij,rjc->ric", mixing, gate_low, preferred_element_type=wide)
            + bias_rows[None, :, None]
        ).reshape(-1, GATE)
        gated = (left_half * spatial).astype(low_type)
        branch = jnp.dot(gated, weight_out, preferred_element_type=wide) + bias_out
        mixed_rows = (inputs + branch * keep_flat).astype(low_type).reshape(mine, SEQ, D)
        mixed = to_places(mixed_rows)

        grad_branch = back_low.astype(wide).reshape(-1, D) * keep_flat
        grad_bias_out = jnp.sum(grad_branch, 0)
        branch_low = grad_branch.astype(low_type)
        grad_weight_out = jnp.einsum("tg,td->gd", gated, branch_low, preferred_element_type=wide)
        grad_gated = jnp.einsum("td,gd->tg", branch_low, weight_out, preferred_element_type=wide)
        grad_spatial = grad_gated * left_half
        grad_left = grad_gated * spatial
        grad_bias_spatial = jnp.sum(grad_spatial.reshape(mine, SEQ, GATE), (0, 2))
        spatial_low = grad_spatial.astype(low_type).reshape(mine, SEQ, GATE)
        grad_gate = jnp.einsum("rij,ric->rjc", mixing, spatial_low, preferred_element_type=wide)
        products = jnp.einsum("ric,rjc->rij", spatial_low, gate_low, preferred_element_type=wide)
        grad_weight_spatial = jnp.sum(jnp.where(same_rows, products, 0.0), 0)
        grad_gate = grad_gate.reshape(-1, GATE)
        grad_gain_gate = jnp.sum(grad_gate * normed_gate, 0)
        grad_bias_gate = jnp.sum(grad_gate, 0)

        grad_rest = jnp.concatenate(
            [
                relative(relative(grad_weight_spatial, 0), 1)
                .astype(low_type)
                .reshape(devices, spatial_rows, D),
                grad_weight_out.astype(low_type).reshape(devices, -1, D),
            ],
            1,
        )
        rest_sum = reduce_blocks(grad_rest.reshape(-1, D), sizes, place)

        grad_right = norm_back(grad_gate * gain_gate, normed_gate, inverse_gate)
        grad_hidden = jnp.concatenate([grad_left, grad_right], 1)
        grad_pre = gelu_back(grad_hidden)[0]
        grad_bias_hidden = jnp.sum(grad_pre, 0)
        pre_low = grad_pre.astype(low_type)
        grad_weight_in = jnp.einsum("td,th->dh", scaled_in, pre_low, preferred_element_type=wide)
        grad_scaled = jnp.einsum("th,dh->td", pre_low, weight_in, preferred_element_type=wide)
        grad_gain_in = jnp.sum(grad_scaled * normed_in, 0)
        grad_bias_in = jnp.sum(grad_scaled, 0)
        branch_grad = norm_back(grad_scaled * gain_in, normed_in, inverse_in)
        branch_grad = branch_grad.astype(low_type).reshape(mine, SEQ, D)
        input_grad = cotangent.astype(wide) + to_places(branch_grad).astype(wide)

        grad_vector = jnp.concatenate(
            [
                grad_gain_in,
                grad_bias_in,
                grad_bias_hidden,
                grad_gain_gate,
                grad_bias_gate,
                relative(grad_bias_spatial, 0),
                grad_bias_out,
            ]
        )
        vector_part = grad_vector.astype(low_type).reshape(in_rows * devices, -1)
        vector_part = jnp.pad(vector_part, ((0, 0), (0, LANE - vector_cols)))
        in_part = grad_weight_in.astype(low_type).reshape(in_rows * devices, -1)
        in_sum = reduce_blocks(jnp.concatenate([in_part, vector_part], 1), sizes, place)

        shards = (
            in_sum[:, :in_width].reshape(-1).astype(wide),
            rest_sum[:spatial_rows].reshape(-1).astype(wide),
            rest_sum[spatial_rows:].reshape(-1).astype(wide),
            in_sum[:, in_width : in_width + vector_cols].reshape(-1).astype(wide),
        )
        in_new = adamw(in_master, in_first, in_second, shards[0], rate_in, decay_matrix)
        spatial_new = adamw(
            spatial_master, spatial_first, spatial_second, shards[1], rate_spatial, decay_matrix
        )
        out_new = adamw(out_master, out_first, out_second, shards[2], rate_out, decay_matrix)
        vector_new = adamw(vector_master, vector_first, vector_second, shards[3], rate_vector, 0.0)
        return (
            mixed,
            input_grad,
            in_new[0],
            in_new[1],
            in_new[2],
            spatial_new[0],
            spatial_new[1],
            spatial_new[2],
            out_new[0],
            out_new[1],
            out_new[2],
            vector_new[0],
            vector_new[1],
            vector_new[2],
        )

    return local


def solution(mesh):
    sizes = (mesh.shape["batch"], mesh.shape["pos"])
    flat = P(("batch", "pos"))
    acts = P("batch", "pos", None)
    placed = (acts, acts, P("batch", None), P("batch", None), P("batch")) + (flat,) * 12
    return jax.shard_map(
        local_fn(sizes),
        mesh=mesh,
        in_specs=placed,
        out_specs=(acts, acts) + (flat,) * 12,
        check_vma=False,
    )
```

```python
import functools
import math

import jax
import jax.numpy as jnp
from jax import lax
from jax.experimental import pallas as pl
from jax.experimental.pallas import tpu as pltpu
from jax.sharding import PartitionSpec as P

D = 512
HID = 3072
SEQ = 512
GATE = 1536
LANE = 128

norm_eps = 1e-05
beta_one = 0.9
beta_two = 0.999
adam_eps = 1e-08
step_count = 10.0
decay_matrix = 0.1
rate_in = 0.12
rate_spatial = 0.2
rate_out = 0.07
rate_vector = 1.0

low_type = jnp.bfloat16
wide = jnp.float32


def split_vector(vector):
    lengths = [D, D, HID, GATE, GATE, SEQ, D]
    pieces = []
    cursor = 0
    for length in lengths:
        pieces.append(vector[cursor : cursor + length])
        cursor = cursor + length
    return pieces


def norm_parts(values):
    average = jnp.mean(values, -1, keepdims=True)
    centred = values - average
    spread = jnp.mean(centred * centred, -1, keepdims=True)
    inverse = lax.rsqrt(spread + norm_eps)
    return (centred * inverse, inverse)


def norm_back(grad_hat, normed, inverse):
    first_mean = jnp.mean(grad_hat, -1, keepdims=True)
    cross_mean = jnp.mean(grad_hat * normed, -1, keepdims=True)
    return (grad_hat - first_mean - normed * cross_mean) * inverse


def adamw(master, first, second, gradient, rate, decay):
    first_new = beta_one * first + (1.0 - beta_one) * gradient
    second_new = beta_two * second + (1.0 - beta_two) * gradient * gradient
    first_hat = first_new / (1.0 - beta_one**step_count)
    second_hat = second_new / (1.0 - beta_two**step_count)
    master_new = master - rate * (first_hat / (jnp.sqrt(second_hat) + adam_eps) + decay * master)
    return (master_new, first_new, second_new)


def swap(value, axis, size, mask):
    return lax.ppermute(value, axis, [(i, i ^ mask) for i in range(size)])


def bit_count(size):
    bits = size.bit_length() - 1
    assert size == 1 << bits
    return bits


def batch_rounds(bits):
    if bits == 3:
        return [(1, 2), (0,)]
    return [(b,) for b in range(1, bits)] + [(0,)]


def gather_blocks(block, sizes, place):
    batch_size, pos_size = sizes
    b, z = place
    rows, cols = block.shape
    bits = bit_count(batch_size)
    zbits = bit_count(pos_size)
    total = bits + zbits
    held = block.reshape((1,) * total + (rows, cols))

    def exchange(held, axis_name, size, index, group, shift):
        pieces = [held]
        for g in range(1, 1 << len(group)):
            mask = sum((1 << group[i]) for i in range(len(group)) if (g >> i) & 1)
            pieces.append(swap(held, axis_name, size, mask))
        for bit in group:
            axis = total - 1 - (bit + shift)
            mine = (index >> bit) & 1
            merged = []
            for a, c in zip(pieces[0::2], pieces[1::2]):
                merged.append(
                    jnp.where(
                        mine == 0,
                        jnp.concatenate([a, c], axis),
                        jnp.concatenate([c, a], axis),
                    )
                )
            pieces = merged
        return pieces[0]

    for bit in reversed(range(zbits)):
        held = exchange(held, "pos", pos_size, z, (bit,), 0)
    for group in batch_rounds(bits):
        held = exchange(held, "batch", batch_size, b, group, zbits)
    return held.reshape(batch_size * pos_size * rows, cols)


def reduce_blocks(grad, sizes, place):
    batch_size, pos_size = sizes
    b, z = place
    bits = bit_count(batch_size)
    zbits = bit_count(pos_size)
    total = bits + zbits
    cols = grad.shape[1]
    rows = grad.shape[0] // (batch_size * pos_size)
    held = grad.reshape((2,) * total + (rows, cols))

    def halve(held, axis_name, size, index, group, shift):
        parts = {0: held}
        for i, bit in enumerate(group):
            axis = total - 1 - (bit + shift)
            mine = (index >> bit) & 1
            spread = {}
            for g, part in parts.items():
                spread[g] = lax.dynamic_slice_in_dim(part, mine, 1, axis)
                spread[g | (1 << i)] = lax.dynamic_slice_in_dim(part, 1 - mine, 1, axis)
            parts = spread
        summed = parts[0].astype(wide)
        for g, part in parts.items():
            if g:
                mask = sum((1 << group[i]) for i in range(len(group)) if (g >> i) & 1)
                summed = summed + swap(part, axis_name, size, mask).astype(wide)
        return summed.astype(grad.dtype)

    for group in reversed(batch_rounds(bits)):
        held = halve(held, "batch", batch_size, b, group, zbits)
    for bit in range(zbits):
        held = halve(held, "pos", pos_size, z, (bit,), 0)
    return held.reshape(rows, cols)


CHUNK = 512
TILE = 256

tail_slope = 0.39 / math.sqrt(2.0)
tail_series = (
    0.23532609033994684,
    0.09138275083966492,
    0.6495739793206253,
    -0.6354188599562557,
    0.8866760936996321,
    -0.22754005589281026,
)
exp_scale = -0.5 / math.log(2.0)
density = 1.0 / math.sqrt(2.0 * math.pi)


def gelu_and_slope(v):
    size = jnp.abs(v)
    t = 1.0 / (1.0 + tail_slope * size)
    bell = jnp.exp2(exp_scale * (v * v))
    series = 0.5 * tail_series[-1]
    for c in reversed(tail_series[:-1]):
        series = series * t + 0.5 * c
    tail = series * t * bell
    phi = jnp.where(v > 0, 1.0 - tail, tail)
    return v * phi, phi + (density * v) * bell


def dot(a, b, ca=1, cb=0):
    return lax.dot_general(a, b, (((ca,), (cb,)), ((), ())), preferred_element_type=wide)


def project_kernel(
    x_ref, w_ref, gain_in, bias_in, bias_hidden, gain_gate, bias_gate,
    scaled_ref, left_ref, slope_ref, normed_ref, inverse_ref, gate_ref, half_ref,
):
    normed, _ = norm_parts(x_ref[...].astype(wide))
    scaled = (normed * gain_in[...] + bias_in[...]).astype(low_type)
    scaled_ref[...] = scaled

    def part(step, base, out):
        at = pl.multiple_of(step * CHUNK, CHUNK)
        cols = pl.ds(pl.multiple_of(base + at, CHUNK), CHUNK)
        value, slope = gelu_and_slope(dot(scaled, w_ref[:, cols]) + bias_hidden[:, cols])
        slope_ref[:, cols] = slope.astype(low_type)
        out[:, pl.ds(at, CHUNK)] = value.astype(out.dtype)

    def body(step, carry):
        part(step, 0, left_ref)
        part(step, GATE, half_ref)
        return carry

    lax.fori_loop(0, GATE // CHUNK, body, 0)
    normed_gate, inverse = norm_parts(half_ref[...])
    inverse_ref[...] = inverse
    normed_ref[...] = normed_gate.astype(low_type)
    gate_ref[...] = (normed_gate * gain_gate[...] + bias_gate[...]).astype(low_type)


def mix_kernel(
    x_ref, own_ref, key_ref, keep_ref, ws_ref, wo_ref, bias_s, bias_o, left_ref, gate_ref,
    mixed_ref, spatial_ref, gated_ref,
):
    same = own_ref[0] == key_ref[0]
    mixing = jnp.where(same, ws_ref[...].astype(wide), 0.0).astype(low_type)
    branch = jnp.zeros(x_ref.shape[1:], wide)
    for c in range(GATE // CHUNK):
        cols = slice(c * CHUNK, (c + 1) * CHUNK)
        spatial = dot(mixing, gate_ref[0, :, cols]) + bias_s[...]
        gated = (left_ref[0, :, cols].astype(wide) * spatial).astype(low_type)
        spatial_ref[0, :, cols] = spatial.astype(low_type)
        gated_ref[0, :, cols] = gated
        branch = branch + dot(gated, wo_ref[cols, :])
    mixed = x_ref[0].astype(wide) + keep_ref[0] * (branch + bias_o[...])
    mixed_ref[0] = mixed.astype(low_type)


def back_kernel(
    cot_ref, own_ref, key_ref, own_line, key_line, keep_ref, ws_ref, wst_ref, wo_ref, gain_gate,
    left_ref, gate_ref, normed_ref, inverse_ref, spatial_ref, gated_ref, slope_ref,
    pre_ref, dwo_ref, dws_ref, dbo_ref, dbs_ref, dgain_ref, dbias_ref, dbh_ref,
    dwo_acc, dws_acc, gate_acc,
):
    row = pl.program_id(0)

    @pl.when(row == 0)
    def _():
        for ref in (dwo_acc, dws_acc, dbo_ref, dbs_ref, dgain_ref, dbias_ref, dbh_ref):
            ref[...] = jnp.zeros_like(ref)

    same = own_ref[0] == key_line[0]
    mixing_back = jnp.where(
        own_line[0] == key_ref[0], wst_ref[...].astype(wide), 0.0
    ).astype(low_type)
    grad_branch = cot_ref[0].astype(wide) * keep_ref[0]
    dbo_ref[...] += jnp.sum(grad_branch, 0, keepdims=True)
    branch_low = grad_branch.astype(low_type)
    length = branch_low.shape[0]
    products = jnp.zeros((length, length), wide)
    first = jnp.zeros((length, 1), wide)
    cross = jnp.zeros((length, 1), wide)
    for c in range(GATE // CHUNK):
        cols = slice(c * CHUNK, (c + 1) * CHUNK)
        grad_gated = dot(branch_low, wo_ref[cols, :], 1, 1)
        dwo_acc[cols, :] += dot(gated_ref[0, :, cols], branch_low, 0, 0)
        grad_spatial = grad_gated * left_ref[0, :, cols].astype(wide)
        spatial_low = grad_spatial.astype(low_type)
        dbs_ref[...] += jnp.sum(grad_spatial, 1, keepdims=True)
        pre = (grad_gated * spatial_ref[0, :, cols].astype(wide)) * slope_ref[0, :, cols].astype(wide)
        pre_ref[0, :, cols] = pre.astype(low_type)
        dbh_ref[:, cols] += jnp.sum(pre, 0, keepdims=True)
        products = products + dot(spatial_low, gate_ref[0, :, cols], 1, 1)
        grad_gate = dot(mixing_back, spatial_low)
        normed = normed_ref[0, :, cols].astype(wide)
        dgain_ref[:, cols] += jnp.sum(grad_gate * normed, 0, keepdims=True)
        dbias_ref[:, cols] += jnp.sum(grad_gate, 0, keepdims=True)
        grad_hat = grad_gate * gain_gate[:, cols]
        gate_acc[:, cols] = grad_hat
        first = first + jnp.sum(grad_hat, 1, keepdims=True)
        cross = cross + jnp.sum(grad_hat * normed, 1, keepdims=True)
    dws_acc[...] += jnp.where(same, products, 0.0)
    first = first * (1.0 / GATE)
    cross = cross * (1.0 / GATE)
    inverse = inverse_ref[0]
    for c in range(GATE // CHUNK):
        cols = slice(c * CHUNK, (c + 1) * CHUNK)
        rest = slice(GATE + c * CHUNK, GATE + (c + 1) * CHUNK)
        normed = normed_ref[0, :, cols].astype(wide)
        grad_right = (gate_acc[:, cols] - first - normed * cross) * inverse
        pre = grad_right * slope_ref[0, :, rest].astype(wide)
        pre_ref[0, :, rest] = pre.astype(low_type)
        dbh_ref[:, rest] += jnp.sum(pre, 0, keepdims=True)

    @pl.when(row == pl.num_programs(0) - 1)
    def _():
        dwo_ref[...] = dwo_acc[...].astype(low_type)
        dws_ref[...] = dws_acc[...].astype(low_type)


def whole(*shape):
    return pl.BlockSpec(shape, lambda r: (0,) * len(shape))


def per_row(*shape):
    return pl.BlockSpec((1,) + shape, lambda r: (r,) + (0,) * len(shape))


def shaped(dtype, *shape):
    return jax.ShapeDtypeStruct(shape, dtype)


def project(x, weight_in, gain_in, bias_in, bias_hidden, gain_gate, bias_gate):
    total = x.shape[0]
    tile = min(TILE, total)
    block = lambda n: pl.BlockSpec((tile, n), lambda i: (i, 0))
    return pl.pallas_call(
        project_kernel,
        grid=(total // tile,),
        in_specs=[block(D), whole(D, HID), whole(1, D), whole(1, D), whole(1, HID), whole(1, GATE), whole(1, GATE)],
        out_specs=[block(D), block(GATE), block(HID), block(GATE), block(1), block(GATE)],
        out_shape=[
            shaped(low_type, total, D),
            shaped(low_type, total, GATE),
            shaped(low_type, total, HID),
            shaped(low_type, total, GATE),
            shaped(wide, total, 1),
            shaped(low_type, total, GATE),
        ],
        scratch_shapes=[pltpu.VMEM((tile, GATE), wide)],
        cost_estimate=pl.CostEstimate(
            flops=2 * total * D * HID + 40 * total * HID, transcendentals=2 * total * HID, bytes_accessed=20 << 20
        ),
        name="project",
    )(x, weight_in, gain_in, bias_in, bias_hidden, gain_gate, bias_gate)


def mix(x, own, key, keep, ws, wo, bias_s, bias_o, left, gate):
    rows, length, _ = x.shape
    return pl.pallas_call(
        mix_kernel,
        grid=(rows,),
        in_specs=[
            per_row(length, D), per_row(length, 1), per_row(1, length), per_row(length, 1),
            whole(length, length), whole(GATE, D), whole(length, 1), whole(1, D),
            per_row(length, GATE), per_row(length, GATE),
        ],
        out_specs=[per_row(length, D), per_row(length, GATE), per_row(length, GATE)],
        out_shape=[
            shaped(low_type, rows, length, D),
            shaped(low_type, rows, length, GATE),
            shaped(low_type, rows, length, GATE),
        ],
        cost_estimate=pl.CostEstimate(
            flops=4 * rows * length * GATE * D, transcendentals=0, bytes_accessed=16 << 20
        ),
        name="mix",
    )(x, own, key, keep, ws, wo, bias_s, bias_o, left, gate)


def back(cot, own, key, keep, ws, wst, wo, gain_gate, left, gate, normed, inverse, spatial, gated, slope):
    rows, length, _ = cot.shape
    own_line = own.reshape(rows, 1, length)
    key_col = key.reshape(rows, length, 1)
    return pl.pallas_call(
        back_kernel,
        grid=(rows,),
        in_specs=[
            per_row(length, D), per_row(length, 1), per_row(length, 1), per_row(1, length), per_row(1, length),
            per_row(length, 1), whole(length, length), whole(length, length), whole(GATE, D), whole(1, GATE),
            per_row(length, GATE), per_row(length, GATE), per_row(length, GATE), per_row(length, 1),
            per_row(length, GATE), per_row(length, GATE), per_row(length, HID),
        ],
        out_specs=[
            per_row(length, HID), whole(GATE, D), whole(length, length), whole(1, D), whole(length, 1),
            whole(1, GATE), whole(1, GATE), whole(1, HID),
        ],
        out_shape=[
            shaped(low_type, rows, length, HID),
            shaped(low_type, GATE, D),
            shaped(low_type, length, length),
            shaped(wide, 1, D),
            shaped(wide, length, 1),
            shaped(wide, 1, GATE),
            shaped(wide, 1, GATE),
            shaped(wide, 1, HID),
        ],
        scratch_shapes=[
            pltpu.VMEM((GATE, D), wide),
            pltpu.VMEM((length, length), wide),
            pltpu.VMEM((length, GATE), wide),
        ],
        cost_estimate=pl.CostEstimate(
            flops=8 * rows * length * GATE * D, transcendentals=0, bytes_accessed=30 << 20
        ),
        name="back",
    )(cot, own, key_col, own_line, key, keep, ws, wst, wo, gain_gate, left, gate, normed, inverse, spatial, gated, slope)


def local_fn(sizes):
    batch_size, pos_size = sizes

    def local(
        tokens,
        cotangent,
        segment_ids,
        pad_mask,
        skip_flags,
        in_master,
        spatial_master,
        out_master,
        vector_master,
        in_first,
        spatial_first,
        out_first,
        vector_first,
        in_second,
        spatial_second,
        out_second,
        vector_second,
    ):
        b = lax.axis_index("batch")
        z = lax.axis_index("pos")
        place = (b, z)
        devices = batch_size * pos_size
        rows = tokens.shape[0]
        length = tokens.shape[1]
        mine = rows // pos_size

        def relative(value, axis):
            return jnp.concatenate(
                [
                    lax.dynamic_slice_in_dim(
                        value, (z ^ k) * (value.shape[axis] // pos_size), value.shape[axis] // pos_size, axis
                    )
                    for k in range(pos_size)
                ],
                axis,
            )

        def to_rows(value):
            parts = []
            for k in range(pos_size):
                part = lax.dynamic_slice_in_dim(value, (z ^ k) * mine, mine, 0)
                parts.append(part if k == 0 else swap(part, "pos", pos_size, k))
            return jnp.concatenate(parts, 1)

        def to_places(value):
            parts = []
            for k in range(pos_size):
                part = lax.slice_in_dim(value, k * length, (k + 1) * length, axis=1)
                parts.append(part if k == 0 else swap(part, "pos", pos_size, k))
            return relative(jnp.concatenate(parts, 0), 0)

        in_rows = D // devices if D % devices == 0 else 1
        in_block = in_master.astype(low_type).reshape(in_rows, -1)
        vector_block = vector_master.astype(low_type).reshape(in_rows, -1)
        vector_cols = vector_block.shape[1]
        vector_block = jnp.pad(vector_block, ((0, 0), (0, LANE - vector_cols)))
        in_block = jnp.concatenate([in_block, vector_block], 1)
        spatial_block = spatial_master.astype(low_type).reshape(-1, D)
        out_block = out_master.astype(low_type).reshape(-1, D)
        rest_block = jnp.concatenate([spatial_block, out_block], 0)
        spatial_rows = spatial_block.shape[0]
        in_width = in_master.shape[0] // in_rows

        in_all = gather_blocks(in_block, sizes, place)
        inputs_low = to_rows(tokens)
        rest_all = gather_blocks(rest_block, sizes, place).reshape(devices, -1, D)
        back_low = to_rows(cotangent)

        weight_in = in_all[:, :in_width].reshape(D, HID)
        vector_flat = in_all[:, in_width : in_width + vector_cols].reshape(-1)
        weight_spatial = rest_all[:, :spatial_rows].reshape(SEQ, SEQ)
        weight_out = rest_all[:, spatial_rows:].reshape(GATE, D)
        gain_in, bias_in, bias_hidden, gain_gate, bias_gate, bias_spatial, bias_out = split_vector(
            vector_flat.astype(wide)
        )

        own_rows = lambda value: lax.dynamic_slice_in_dim(value, z * mine, mine, 0)
        segments = relative(own_rows(segment_ids), 1)
        padding = relative(own_rows(pad_mask), 1)
        keep = padding.astype(wide) * (1.0 - own_rows(skip_flags).astype(wide))[:, None]
        keep = keep[:, :, None]
        own = segments[:, :, None]
        key = jnp.where(padding == 1, segments, -1)[:, None, :]
        mixing_rows = relative(relative(weight_spatial, 0), 1)
        bias_rows = relative(bias_spatial, 0)[:, None]

        scaled_in, left_half, slope, normed_gate, inverse_gate, gate_low = project(
            inputs_low.reshape(-1, D),
            weight_in,
            gain_in[None],
            bias_in[None],
            bias_hidden[None],
            gain_gate[None],
            bias_gate[None],
        )
        by_row = lambda value: value.reshape(mine, SEQ, -1)
        left_half, slope, normed_gate, inverse_gate, gate_low = map(
            by_row, (left_half, slope, normed_gate, inverse_gate, gate_low)
        )
        mixed_rows, spatial, gated = mix(
            inputs_low, own, key, keep, mixing_rows, weight_out, bias_rows, bias_out[None], left_half, gate_low
        )
        mixed = to_places(mixed_rows)
        (
            pre_low,
            grad_weight_out,
            grad_weight_spatial,
            grad_bias_out,
            grad_bias_spatial,
            grad_gain_gate,
            grad_bias_gate,
            grad_bias_hidden,
        ) = back(
            back_low, own, key, keep, mixing_rows, mixing_rows.T, weight_out, gain_gate[None],
            left_half, gate_low, normed_gate, inverse_gate, spatial, gated, slope,
        )
        pre_low = pre_low.reshape(-1, HID)

        grad_rest = jnp.concatenate(
            [
                relative(relative(grad_weight_spatial, 0), 1)
                .astype(low_type)
                .reshape(devices, spatial_rows, D),
                grad_weight_out.astype(low_type).reshape(devices, -1, D),
            ],
            1,
        )
        rest_sum = reduce_blocks(grad_rest.reshape(-1, D), sizes, place)

        normed_in, inverse_in = norm_parts(inputs_low.astype(wide).reshape(-1, D))
        grad_weight_in = jnp.einsum("td,th->dh", scaled_in, pre_low, preferred_element_type=wide)
        grad_scaled = jnp.einsum("th,dh->td", pre_low, weight_in, preferred_element_type=wide)
        grad_gain_in = jnp.sum(grad_scaled * normed_in, 0)
        grad_bias_in = jnp.sum(grad_scaled, 0)
        branch_grad = norm_back(grad_scaled * gain_in, normed_in, inverse_in)
        branch_grad = branch_grad.astype(low_type).reshape(mine, SEQ, D)
        input_grad = cotangent.astype(wide) + to_places(branch_grad).astype(wide)

        grad_vector = jnp.concatenate(
            [
                grad_gain_in,
                grad_bias_in,
                grad_bias_hidden[0],
                grad_gain_gate[0],
                grad_bias_gate[0],
                relative(grad_bias_spatial[:, 0], 0),
                grad_bias_out[0],
            ]
        )
        vector_part = grad_vector.astype(low_type).reshape(in_rows * devices, -1)
        vector_part = jnp.pad(vector_part, ((0, 0), (0, LANE - vector_cols)))
        in_part = grad_weight_in.astype(low_type).reshape(in_rows * devices, -1)
        in_sum = reduce_blocks(jnp.concatenate([in_part, vector_part], 1), sizes, place)

        shards = (
            in_sum[:, :in_width].reshape(-1).astype(wide),
            rest_sum[:spatial_rows].reshape(-1).astype(wide),
            rest_sum[spatial_rows:].reshape(-1).astype(wide),
            in_sum[:, in_width : in_width + vector_cols].reshape(-1).astype(wide),
        )
        in_new = adamw(in_master, in_first, in_second, shards[0], rate_in, decay_matrix)
        spatial_new = adamw(
            spatial_master, spatial_first, spatial_second, shards[1], rate_spatial, decay_matrix
        )
        out_new = adamw(out_master, out_first, out_second, shards[2], rate_out, decay_matrix)
        vector_new = adamw(vector_master, vector_first, vector_second, shards[3], rate_vector, 0.0)
        return (
            mixed,
            input_grad,
            in_new[0],
            in_new[1],
            in_new[2],
            spatial_new[0],
            spatial_new[1],
            spatial_new[2],
            out_new[0],
            out_new[1],
            out_new[2],
            vector_new[0],
            vector_new[1],
            vector_new[2],
        )

    return local


def solution(mesh):
    sizes = (mesh.shape["batch"], mesh.shape["pos"])
    flat = P(("batch", "pos"))
    acts = P("batch", "pos", None)
    placed = (acts, acts, P("batch", None), P("batch", None), P("batch")) + (flat,) * 12
    return jax.shard_map(
        local_fn(sizes),
        mesh=mesh,
        in_specs=placed,
        out_specs=(acts, acts) + (flat,) * 12,
        check_vma=False,
    )
```

```python
import functools
import math

import jax
import jax.numpy as jnp
from jax import lax
from jax.experimental import pallas as pl
from jax.experimental.pallas import tpu as pltpu
from jax.sharding import PartitionSpec as P


D = 512
HID = 3072
SEQ = 512
GATE = 1536
LANE = 128

norm_eps = 1e-05
beta_one = 0.9
beta_two = 0.999
adam_eps = 1e-08
step_count = 10.0
decay_matrix = 0.1
rate_in = 0.12
rate_spatial = 0.2
rate_out = 0.07
rate_vector = 1.0

low_type = jnp.bfloat16
wide = jnp.float32


def norm_parts(values):
    average = jnp.mean(values, -1, keepdims=True)
    centred = values - average
    spread = jnp.mean(centred * centred, -1, keepdims=True)
    inverse = lax.rsqrt(spread + norm_eps)
    return (centred * inverse, inverse)


def norm_back(grad_hat, normed, inverse):
    first_mean = jnp.mean(grad_hat, -1, keepdims=True)
    cross_mean = jnp.mean(grad_hat * normed, -1, keepdims=True)
    return (grad_hat - first_mean - normed * cross_mean) * inverse


def adamw(master, first, second, gradient, rate, decay):
    first_new = beta_one * first + (1.0 - beta_one) * gradient
    second_new = beta_two * second + (1.0 - beta_two) * gradient * gradient
    first_hat = first_new / (1.0 - beta_one**step_count)
    second_hat = second_new / (1.0 - beta_two**step_count)
    master_new = master - rate * (first_hat / (jnp.sqrt(second_hat) + adam_eps) + decay * master)
    return (master_new, first_new, second_new)


def swap(value, axis, size, mask):
    return lax.ppermute(value, axis, [(i, i ^ mask) for i in range(size)])


def bit_count(size):
    bits = size.bit_length() - 1
    assert size == 1 << bits
    return bits


def batch_rounds(bits):
    if bits == 3:
        return [(1, 2), (0,)]
    return [(b,) for b in range(1, bits)] + [(0,)]


def gather_blocks(block, sizes, place):
    batch_size, pos_size = sizes
    b, z = place
    rows, cols = block.shape
    bits = bit_count(batch_size)
    zbits = bit_count(pos_size)
    total = bits + zbits
    held = block.reshape((1,) * total + (rows, cols))

    def exchange(held, axis_name, size, index, group, shift):
        pieces = [held]
        for g in range(1, 1 << len(group)):
            mask = sum((1 << group[i]) for i in range(len(group)) if (g >> i) & 1)
            pieces.append(swap(held, axis_name, size, mask))
        for bit in group:
            axis = total - 1 - (bit + shift)
            mine = (index >> bit) & 1
            merged = []
            for a, c in zip(pieces[0::2], pieces[1::2]):
                merged.append(
                    jnp.where(
                        mine == 0,
                        jnp.concatenate([a, c], axis),
                        jnp.concatenate([c, a], axis),
                    )
                )
            pieces = merged
        return pieces[0]

    for bit in reversed(range(zbits)):
        held = exchange(held, "pos", pos_size, z, (bit,), 0)
    for group in batch_rounds(bits):
        held = exchange(held, "batch", batch_size, b, group, zbits)
    return held.reshape(batch_size * pos_size * rows, cols)


def reduce_blocks(grad, sizes, place, late=None):
    batch_size, pos_size = sizes
    b, z = place
    bits = bit_count(batch_size)
    zbits = bit_count(pos_size)
    total = bits + zbits
    rows = grad.shape[0] // (batch_size * pos_size)
    held = grad.reshape((2,) * total + (rows, -1))
    if late is not None:
        late = late.reshape((2,) * total + (rows, -1))

    def halve(held, axis_name, size, index, group, shift):
        parts = {0: held}
        for i, bit in enumerate(group):
            axis = total - 1 - (bit + shift)
            mine = (index >> bit) & 1
            spread = {}
            for g, part in parts.items():
                spread[g] = lax.dynamic_slice_in_dim(part, mine, 1, axis)
                spread[g | (1 << i)] = lax.dynamic_slice_in_dim(part, 1 - mine, 1, axis)
            parts = spread
        summed = parts[0].astype(wide)
        for g, part in parts.items():
            if g:
                mask = sum((1 << group[i]) for i in range(len(group)) if (g >> i) & 1)
                summed = summed + swap(part, axis_name, size, mask).astype(wide)
        return summed.astype(grad.dtype)

    for group in reversed(batch_rounds(bits)):
        held = halve(held, "batch", batch_size, b, group, zbits)
        if late is not None:
            late = halve(late, "batch", batch_size, b, group, zbits)
            held = jnp.concatenate([held, late], total + 1)
            late = None
    for bit in range(zbits):
        held = halve(held, "pos", pos_size, z, (bit,), 0)
    return held.reshape(rows, -1)


CHUNK = 512

lengths = (D, D, HID, GATE, GATE, SEQ, D)
ends = [sum(lengths[: i + 1]) for i in range(len(lengths))]
GAIN_IN, BIAS_IN, BIAS_HIDDEN, GAIN_GATE, BIAS_GATE, BIAS_SPATIAL, BIAS_OUT = (
    slice(end - n, end) for end, n in zip(ends, lengths)
)
VEC = ends[-1]


def shifted(outer, inner):
    return slice(outer.start + inner.start, outer.start + inner.stop)


tail_slope = 0.39 / math.sqrt(2.0)
tail_series = (
    0.23532609033994684,
    0.09138275083966492,
    0.6495739793206253,
    -0.6354188599562557,
    0.8866760936996321,
    -0.22754005589281026,
)
exp_scale = -0.5 / math.log(2.0)
density = 1.0 / math.sqrt(2.0 * math.pi)


def gelu_and_slope(v):
    size = jnp.abs(v)
    t = 1.0 / (1.0 + tail_slope * size)
    bell = jnp.exp2(exp_scale * (v * v))
    series = 0.5 * tail_series[-1]
    for c in reversed(tail_series[:-1]):
        series = series * t + 0.5 * c
    tail = series * t * bell
    phi = jnp.where(v > 0, 1.0 - tail, tail)
    return v * phi, phi + (density * v) * bell


def dot(a, b, ca=1, cb=0):
    return lax.dot_general(a, b, (((ca,), (cb,)), ((), ())), preferred_element_type=wide)


def column_blocks(k):
    return slice(k * CHUNK, (k + 1) * CHUNK)


def block_at(z, k, size, base=0):
    return pl.ds(pl.multiple_of(base + (z ^ k) * size, LANE), size)


def project_kernel(pos_size, *refs):
    pieces = refs[:pos_size]
    (w_ref, vec, x_ref, scaled_ref, left_ref, slope_ref, normed_ref, inverse_ref, gate_ref, half_ref) = refs[
        pos_size:
    ]
    mine, _, length, _ = x_ref.shape
    total = mine * length
    for k in range(pos_size):

        @pl.when(pl.program_id(0) == k)
        def _():
            x_ref[:, 0] = pieces[k][...]

    normed, _ = norm_parts(x_ref[:, 0].reshape(total, D).astype(wide))
    scaled = (normed * vec[:, GAIN_IN] + vec[:, BIAS_IN]).astype(low_type)
    scaled_ref[:, 0] = scaled.reshape(mine, length, D)

    def part(step, base):
        at = pl.multiple_of(step * CHUNK, CHUNK)
        cols = pl.ds(pl.multiple_of(base + at, CHUNK), CHUNK)
        bias = vec[:, pl.ds(pl.multiple_of(BIAS_HIDDEN.start + base + at, CHUNK), CHUNK)]
        value, slope = gelu_and_slope(dot(scaled, w_ref[:, cols]) + bias)
        slope_ref[:, 0, :, cols] = slope.astype(low_type).reshape(mine, length, CHUNK)
        return pl.ds(at, CHUNK), value

    def body(step, carry):
        cols, value = part(step, 0)
        left_ref[:, 0, :, cols] = value.astype(low_type).reshape(mine, length, CHUNK)
        cols, value = part(step, GATE)
        half_ref[:, cols] = value
        return carry

    lax.fori_loop(0, GATE // CHUNK, body, 0)
    normed_gate, inverse = norm_parts(half_ref[...])
    inverse_ref[:, 0] = inverse.reshape(mine, length, 1)
    normed_ref[:, 0] = normed_gate.astype(low_type).reshape(mine, length, GATE)
    gate = (normed_gate * vec[:, GAIN_GATE] + vec[:, BIAS_GATE]).astype(low_type)
    gate_ref[:, 0] = gate.reshape(mine, length, GATE)


def mix_kernel(pos_size, *refs):
    (x_ref, seg_ref, pad_ref, skip_ref, ws_ref, wo_ref, vec, left_ref, gate_ref) = refs[:9]
    mixed_refs = refs[9 : 9 + pos_size]
    spatial_ref, gated_ref, mixing_ref, col_ref, line_ref = refs[9 + pos_size :]
    z = lax.axis_index("pos")
    row = z * pl.num_programs(0) + pl.program_id(0)
    length = x_ref.shape[1]
    part = length // pos_size
    places = range(pos_size)

    def line(ref):
        rows = jnp.concatenate([ref[:, block_at(z, k, part)] for k in places], 1)
        at = lax.broadcasted_iota(jnp.int32, rows.shape, 0)
        return jnp.sum(jnp.where(at == row, rows.astype(wide), 0.0), 0, keepdims=True)

    segment = line(seg_ref)
    padding = line(pad_ref)
    keep = padding * (1.0 - skip_ref[row].astype(wide))
    key = jnp.where(padding == 1.0, segment, -1.0)
    bias = jnp.concatenate([vec[:, block_at(z, k, part, BIAS_SPATIAL.start)] for k in places], 1)
    lines = jnp.concatenate([segment, keep, bias, key, jnp.zeros((4, length), wide)], 0)
    col = lines.T
    line_ref[0] = lines
    col_ref[0] = col
    weights = jnp.concatenate(
        [
            jnp.concatenate([ws_ref[block_at(z, i, part), block_at(z, j, part)] for j in places], 1)
            for i in places
        ],
        0,
    )
    masked = jnp.where(col[:, 0:1] == key, weights.astype(wide), 0.0)
    mixing = masked.astype(low_type)
    mixing_ref[0] = masked.T.astype(low_type)
    branch = jnp.zeros(x_ref.shape[1:], wide)
    for c in range(GATE // CHUNK):
        cols = column_blocks(c)
        spatial = dot(mixing, gate_ref[0, :, cols]) + col[:, 2:3]
        gated = (left_ref[0, :, cols].astype(wide) * spatial).astype(low_type)
        spatial_ref[0, :, cols] = spatial.astype(low_type)
        gated_ref[0, :, cols] = gated
        branch = branch + dot(gated, wo_ref[cols, :])
    mixed = (x_ref[0].astype(wide) + col[:, 1:2] * (branch + vec[:, BIAS_OUT])).astype(low_type)
    for k in places:
        mixed_refs[k][0] = mixed[k * part : (k + 1) * part]


def back_kernel(pos_size, *refs):
    cot_refs = refs[:pos_size]
    (
        col_ref, line_ref, mixing_ref, wo_ref, vec, left_ref, gate_ref, normed_ref, inverse_ref,
        spatial_ref, gated_ref, slope_ref, pre_ref, dwo_ref, dws_ref, dvec, dwo_acc, dws_acc, gate_acc,
    ) = refs[pos_size:]
    row = pl.program_id(0)
    z = lax.axis_index("pos")

    @pl.when(row == 0)
    def _():
        for ref in (dwo_acc, dws_acc, dvec):
            ref[...] = jnp.zeros_like(ref)

    col = col_ref[0]
    same = col[:, 0:1] == line_ref[0][3:4]
    mixing_back = mixing_ref[0]
    cot = jnp.concatenate([ref[0] for ref in cot_refs], 0)
    grad_branch = cot.astype(wide) * col[:, 1:2]
    dvec[:, BIAS_OUT] += jnp.sum(grad_branch, 0, keepdims=True)
    branch_low = grad_branch.astype(low_type)
    length = branch_low.shape[0]
    part = length // pos_size
    products = jnp.zeros((length, length), wide)
    first = jnp.zeros((length, 1), wide)
    cross = jnp.zeros((length, 1), wide)
    spatial_bias = jnp.zeros((8, length), wide)
    ones = jnp.ones((8, CHUNK), low_type)
    for c in range(GATE // CHUNK):
        cols = column_blocks(c)
        grad_gated = dot(branch_low, wo_ref[cols, :], 1, 1)
        dwo_acc[cols, :] += dot(gated_ref[0, :, cols], branch_low, 0, 0)
        spatial_low = (grad_gated * left_ref[0, :, cols].astype(wide)).astype(low_type)
        spatial_bias = spatial_bias + dot(ones, spatial_low, 1, 1)
        pre = (grad_gated * spatial_ref[0, :, cols].astype(wide)) * slope_ref[0, :, cols].astype(wide)
        pre_ref[0, :, cols] = pre.astype(low_type)
        dvec[:, shifted(BIAS_HIDDEN, cols)] += jnp.sum(pre, 0, keepdims=True)
        products = products + dot(spatial_low, gate_ref[0, :, cols], 1, 1)
        grad_gate = dot(mixing_back, spatial_low)
        normed = normed_ref[0, :, cols].astype(wide)
        dvec[:, shifted(GAIN_GATE, cols)] += jnp.sum(grad_gate * normed, 0, keepdims=True)
        dvec[:, shifted(BIAS_GATE, cols)] += jnp.sum(grad_gate, 0, keepdims=True)
        grad_hat = grad_gate * vec[:, shifted(GAIN_GATE, cols)]
        gate_acc[:, cols] = grad_hat
        first = first + jnp.sum(grad_hat, 1, keepdims=True)
        cross = cross + jnp.sum(grad_hat * normed, 1, keepdims=True)
    for k in range(pos_size):
        dvec[:, block_at(z, k, part, BIAS_SPATIAL.start)] += spatial_bias[0:1, k * part : (k + 1) * part]
    dws_acc[...] += jnp.where(same, products, 0.0)
    first = first * (1.0 / GATE)
    cross = cross * (1.0 / GATE)
    inverse = inverse_ref[0]
    for c in range(GATE // CHUNK):
        cols = column_blocks(c)
        rest = shifted(slice(GATE, HID), cols)
        normed = normed_ref[0, :, cols].astype(wide)
        grad_right = (gate_acc[:, cols] - first - normed * cross) * inverse
        pre = grad_right * slope_ref[0, :, rest].astype(wide)
        pre_ref[0, :, rest] = pre.astype(low_type)
        dvec[:, shifted(BIAS_HIDDEN, rest)] += jnp.sum(pre, 0, keepdims=True)

    @pl.when(row == pl.num_programs(0) - 1)
    def _():
        dwo_ref[...] = dwo_acc[...].astype(low_type)
        for i in range(pos_size):
            for j in range(pos_size):
                dws_ref[block_at(z, i, part), block_at(z, j, part)] = dws_acc[
                    i * part : (i + 1) * part, j * part : (j + 1) * part
                ].astype(low_type)


def input_kernel(pos_size, pre_ref, w_ref, x_ref, vec, dvec_in, *refs):
    pieces, dvec = refs[:pos_size], refs[pos_size]
    step = pl.program_id(0)
    mine, _, length, _ = x_ref.shape
    total = mine * length

    @pl.when(step == 0)
    def _():
        dvec[...] = dvec_in[...]

    normed, inverse = norm_parts(x_ref[:, 0].reshape(total, D).astype(wide))
    grad_scaled = dot(pre_ref[:, 0].reshape(total, HID), w_ref[...], 1, 1)
    dvec[:, GAIN_IN] += jnp.sum(grad_scaled * normed, 0, keepdims=True)
    dvec[:, BIAS_IN] += jnp.sum(grad_scaled, 0, keepdims=True)
    grad = norm_back(grad_scaled * vec[:, GAIN_IN], normed, inverse).astype(low_type)
    for k in range(pos_size):

        @pl.when(step == k)
        def _():
            pieces[k][...] = grad.reshape(mine, length, D)


def whole(*shape):
    return pl.BlockSpec(shape, lambda r: (0,) * len(shape))


def per_row(*shape):
    return pl.BlockSpec((1,) + shape, lambda r: (r,) + (0,) * len(shape))


def shaped(dtype, *shape):
    return jax.ShapeDtypeStruct(shape, dtype)


def cost(flops, size, rare=0):
    return pl.CostEstimate(flops=flops, transcendentals=rare, bytes_accessed=size)


def project(pieces, w, vec):
    pos_size = len(pieces)
    mine, length, _ = pieces[0].shape
    block = lambda n: pl.BlockSpec((mine, 1, length, n), lambda i: (0, i, 0, 0))
    out = lambda dtype, n: shaped(dtype, mine, pos_size, length, n)
    total = mine * pos_size * length
    return pl.pallas_call(
        functools.partial(project_kernel, pos_size),
        grid=(pos_size,),
        in_specs=[whole(mine, length, D)] * pos_size + [whole(D, HID), whole(1, VEC)],
        out_specs=[block(D), block(D), block(GATE), block(HID), block(GATE), block(1), block(GATE)],
        out_shape=[
            out(low_type, D), out(low_type, D), out(low_type, GATE), out(low_type, HID),
            out(low_type, GATE), out(wide, 1), out(low_type, GATE),
        ],
        scratch_shapes=[pltpu.VMEM((mine * length, GATE), wide)],
        cost_estimate=cost(2 * total * D * HID + 40 * total * HID, 20 << 20, 2 * total * HID),
        name="project",
    )(*pieces, w, vec)


def mix(pos_size, x, seg, pad, skip, ws, wo, vec, left, gate):
    mine, length, _ = x.shape
    part = length // pos_size
    return pl.pallas_call(
        functools.partial(mix_kernel, pos_size),
        grid=(mine,),
        in_specs=[
            per_row(length, D), whole(*seg.shape), whole(*pad.shape), pl.BlockSpec(memory_space=pltpu.SMEM),
            whole(length, length), whole(GATE, D), whole(1, VEC), per_row(length, GATE), per_row(length, GATE),
        ],
        out_specs=[per_row(part, D)] * pos_size
        + [
            per_row(length, GATE), per_row(length, GATE), per_row(length, length), per_row(length, 8),
            per_row(8, length),
        ],
        out_shape=[shaped(low_type, mine, part, D)] * pos_size
        + [
            shaped(low_type, mine, length, GATE),
            shaped(low_type, mine, length, GATE),
            shaped(low_type, mine, length, length),
            shaped(wide, mine, length, 8),
            shaped(wide, mine, 8, length),
        ],
        cost_estimate=cost(4 * mine * length * GATE * D, 16 << 20),
        name="mix",
    )(x, seg, pad, skip, ws, wo, vec, left, gate)


def back(pieces, col, line, mixing, wo, vec, left, gate, normed, inverse, spatial, gated, slope):
    pos_size = len(pieces)
    mine, part, _ = pieces[0].shape
    length = part * pos_size
    return pl.pallas_call(
        functools.partial(back_kernel, pos_size),
        grid=(mine,),
        in_specs=[per_row(part, D)] * pos_size
        + [
            per_row(length, 8), per_row(8, length), per_row(length, length), whole(GATE, D), whole(1, VEC),
            per_row(length, GATE), per_row(length, GATE), per_row(length, GATE), per_row(length, 1),
            per_row(length, GATE), per_row(length, GATE), per_row(length, HID),
        ],
        out_specs=[per_row(length, HID), whole(GATE, D), whole(length, length), whole(1, VEC)],
        out_shape=[
            shaped(low_type, mine, length, HID),
            shaped(low_type, GATE, D),
            shaped(low_type, length, length),
            shaped(wide, 1, VEC),
        ],
        scratch_shapes=[
            pltpu.VMEM((GATE, D), wide),
            pltpu.VMEM((length, length), wide),
            pltpu.VMEM((length, GATE), wide),
        ],
        cost_estimate=cost(8 * mine * length * GATE * D, 30 << 20),
        name="back",
    )(*pieces, col, line, mixing, wo, vec, left, gate, normed, inverse, spatial, gated, slope)


def input_back(pre, w, x, vec, dvec):
    mine, pos_size, length, _ = x.shape
    block = lambda n: pl.BlockSpec((mine, 1, length, n), lambda i: (0, i, 0, 0))
    return pl.pallas_call(
        functools.partial(input_kernel, pos_size),
        grid=(pos_size,),
        in_specs=[block(HID), whole(D, HID), block(D), whole(1, VEC), whole(1, VEC)],
        out_specs=[whole(mine, length, D)] * pos_size + [whole(1, VEC)],
        out_shape=[shaped(low_type, mine, length, D)] * pos_size + [shaped(wide, 1, VEC)],
        cost_estimate=cost(2 * mine * pos_size * length * D * HID, 12 << 20),
        name="input_back",
    )(pre, w, x, vec, dvec)


def local_fn(sizes):
    batch_size, pos_size = sizes

    def local(
        tokens,
        cotangent,
        segment_ids,
        pad_mask,
        skip_flags,
        in_master,
        spatial_master,
        out_master,
        vector_master,
        in_first,
        spatial_first,
        out_first,
        vector_first,
        in_second,
        spatial_second,
        out_second,
        vector_second,
    ):
        b = lax.axis_index("batch")
        z = lax.axis_index("pos")
        place = (b, z)
        devices = batch_size * pos_size
        rows = tokens.shape[0]
        length = tokens.shape[1]
        mine = rows // pos_size

        def exchange(parts):
            return [part if k == 0 else swap(part, "pos", pos_size, k) for k, part in enumerate(parts)]

        def split_rows(value):
            return [lax.dynamic_slice_in_dim(value, (z ^ k) * mine, mine, 0) for k in range(pos_size)]

        def join_rows(parts):
            for bit in range(bit_count(pos_size)):
                lower = ((z >> bit) & 1) == 0
                parts = [
                    jnp.where(
                        lower, jnp.concatenate([u, v], 0), jnp.concatenate([v, u], 0)
                    )
                    for u, v in zip(parts[0::2], parts[1::2])
                ]
            return parts[0]

        in_rows = D // devices if D % devices == 0 else 1
        in_block = in_master.astype(low_type).reshape(in_rows, -1)
        vector_block = vector_master.astype(low_type).reshape(in_rows, -1)
        vector_cols = vector_block.shape[1]
        vector_block = jnp.pad(vector_block, ((0, 0), (0, LANE - vector_cols)))
        in_block = jnp.concatenate([in_block, vector_block], 1)
        spatial_block = spatial_master.astype(low_type).reshape(-1, D)
        out_block = out_master.astype(low_type).reshape(-1, D)
        rest_block = jnp.concatenate([spatial_block, out_block], 0)
        spatial_rows = spatial_block.shape[0]
        in_width = in_master.shape[0] // in_rows

        in_all = gather_blocks(in_block, sizes, place)
        token_parts = exchange(split_rows(tokens))
        rest_all = gather_blocks(rest_block, sizes, place).reshape(devices, -1, D)
        back_parts = exchange(split_rows(cotangent))

        vec = in_all[:, in_width : in_width + vector_cols].reshape(1, -1).astype(wide)
        weight_spatial = rest_all[:, :spatial_rows].reshape(SEQ, SEQ)
        weight_out = rest_all[:, spatial_rows:].reshape(GATE, D)
        saved = project(token_parts, in_all, vec)
        inputs = saved[0]
        by_row = lambda value: value.reshape(mine, SEQ, -1)
        inputs_low, scaled_in, left_half, slope, normed_gate, inverse_gate, gate_low = map(by_row, saved)
        outs = mix(
            pos_size, inputs_low, segment_ids, pad_mask, skip_flags, weight_spatial, weight_out, vec,
            left_half, gate_low,
        )
        mixed_parts = exchange(outs[:pos_size])
        mixed = join_rows(mixed_parts)
        spatial, gated, mixing, col, line = outs[pos_size:]
        pre_low, grad_weight_out, grad_weight_spatial, grad_vector = back(
            back_parts, col, line, mixing, weight_out, vec, left_half, gate_low, normed_gate,
            inverse_gate, spatial, gated, slope,
        )
        scaled_in = scaled_in.reshape(-1, D)
        pre_low = pre_low.reshape(-1, HID)

        grad_rest = jnp.concatenate(
            [
                grad_weight_spatial.reshape(devices, spatial_rows, D),
                grad_weight_out.reshape(devices, -1, D),
            ],
            1,
        )
        rest_sum = reduce_blocks(grad_rest.reshape(-1, D), sizes, place)

        grad_weight_in = jnp.einsum("td,th->dh", scaled_in, pre_low, preferred_element_type=wide)
        grad_weight_in = grad_weight_in.astype(low_type)
        grad_weight_in, pre_low = lax.optimization_barrier((grad_weight_in, pre_low))
        outs = input_back(
            pre_low.reshape(mine, pos_size, length, HID), in_all, inputs, vec, grad_vector
        )
        grad_parts = exchange(outs[:pos_size])
        input_grad = cotangent.astype(wide) + join_rows(grad_parts).astype(wide)
        grad_vector = outs[pos_size]

        vector_part = grad_vector.astype(low_type).reshape(in_rows * devices, -1)
        vector_part = jnp.pad(vector_part, ((0, 0), (0, LANE - vector_cols)))
        in_part = grad_weight_in.reshape(in_rows * devices, -1)
        in_sum = reduce_blocks(in_part, sizes, place, vector_part)

        shards = (
            in_sum[:, :in_width].reshape(-1).astype(wide),
            rest_sum[:spatial_rows].reshape(-1).astype(wide),
            rest_sum[spatial_rows:].reshape(-1).astype(wide),
            in_sum[:, in_width : in_width + vector_cols].reshape(-1).astype(wide),
        )
        in_new = adamw(in_master, in_first, in_second, shards[0], rate_in, decay_matrix)
        spatial_new = adamw(
            spatial_master, spatial_first, spatial_second, shards[1], rate_spatial, decay_matrix
        )
        out_new = adamw(out_master, out_first, out_second, shards[2], rate_out, decay_matrix)
        vector_new = adamw(vector_master, vector_first, vector_second, shards[3], rate_vector, 0.0)
        return (
            mixed,
            input_grad,
            in_new[0],
            in_new[1],
            in_new[2],
            spatial_new[0],
            spatial_new[1],
            spatial_new[2],
            out_new[0],
            out_new[1],
            out_new[2],
            vector_new[0],
            vector_new[1],
            vector_new[2],
        )

    return local


def solution(mesh):
    sizes = (mesh.shape["batch"], mesh.shape["pos"])
    flat = P(("batch", "pos"))
    acts = P("batch", "pos", None)
    placed = (acts, acts, P("batch", None), P("batch", None), P("batch")) + (flat,) * 12
    return jax.shard_map(
        local_fn(sizes),
        mesh=mesh,
        in_specs=placed,
        out_specs=(acts, acts) + (flat,) * 12,
        check_vma=False,
    )
```

```python
import functools
import math

import jax
import jax.numpy as jnp
from jax import lax
from jax.experimental import pallas as pl
from jax.experimental.pallas import tpu as pltpu
from jax.sharding import PartitionSpec as P


D = 512
HID = 3072
SEQ = 512
GATE = 1536
LANE = 128

norm_eps = 1e-05
beta_one = 0.9
beta_two = 0.999
adam_eps = 1e-08
step_count = 10.0
decay_matrix = 0.1
rate_in = 0.12
rate_spatial = 0.2
rate_out = 0.07
rate_vector = 1.0

low_type = jnp.bfloat16
wide = jnp.float32


def norm_parts(values):
    average = jnp.mean(values, -1, keepdims=True)
    centred = values - average
    spread = jnp.mean(centred * centred, -1, keepdims=True)
    inverse = lax.rsqrt(spread + norm_eps)
    return (centred * inverse, inverse)


def norm_back(grad_hat, normed, inverse):
    first_mean = jnp.mean(grad_hat, -1, keepdims=True)
    cross_mean = jnp.mean(grad_hat * normed, -1, keepdims=True)
    return (grad_hat - first_mean - normed * cross_mean) * inverse


def adamw(master, first, second, gradient, rate, decay):
    first_new = beta_one * first + (1.0 - beta_one) * gradient
    second_new = beta_two * second + (1.0 - beta_two) * gradient * gradient
    first_hat = first_new / (1.0 - beta_one**step_count)
    second_hat = second_new / (1.0 - beta_two**step_count)
    master_new = master - rate * (first_hat / (jnp.sqrt(second_hat) + adam_eps) + decay * master)
    return (master_new, first_new, second_new)


def swap(value, axis, size, mask):
    return lax.ppermute(value, axis, [(i, i ^ mask) for i in range(size)])


def bit_count(size):
    bits = size.bit_length() - 1
    assert size == 1 << bits
    return bits


def batch_rounds(bits):
    if bits == 3:
        return [(1, 2), (0,)]
    return [(b,) for b in range(1, bits)] + [(0,)]


def gather_blocks(block, sizes, place, halves=False):
    batch_size, pos_size = sizes
    b, z = place
    rows, cols = block.shape
    bits = bit_count(batch_size)
    zbits = bit_count(pos_size)
    total = bits + zbits
    held = block.reshape((1,) * total + (rows, cols))

    def exchange(held, axis_name, size, index, group, shift):
        pieces = [held]
        for g in range(1, 1 << len(group)):
            mask = sum((1 << group[i]) for i in range(len(group)) if (g >> i) & 1)
            pieces.append(swap(held, axis_name, size, mask))
        for bit in group:
            axis = total - 1 - (bit + shift)
            mine = (index >> bit) & 1
            merged = []
            for a, c in zip(pieces[0::2], pieces[1::2]):
                merged.append(
                    jnp.where(
                        mine == 0,
                        jnp.concatenate([a, c], axis),
                        jnp.concatenate([c, a], axis),
                    )
                )
            pieces = merged
        return pieces[0]

    for bit in reversed(range(zbits)):
        held = exchange(held, "pos", pos_size, z, (bit,), 0)
    for group in batch_rounds(bits):
        if halves and group == (0,):
            held = lax.optimization_barrier(held.reshape(-1, pos_size * rows, cols))
            return held, swap(held, "batch", batch_size, 1)
        held = exchange(held, "batch", batch_size, b, group, zbits)
    return held.reshape(batch_size * pos_size * rows, cols)


def reduce_blocks(grad, sizes, place, late=None):
    batch_size, pos_size = sizes
    b, z = place
    bits = bit_count(batch_size)
    zbits = bit_count(pos_size)
    total = bits + zbits
    rows = grad.shape[0] // (batch_size * pos_size)
    held = grad.reshape((2,) * total + (rows, -1))
    if late is not None:
        late = late.reshape((2,) * total + (rows, -1))

    def halve(held, axis_name, size, index, group, shift):
        parts = {0: held}
        for i, bit in enumerate(group):
            axis = total - 1 - (bit + shift)
            mine = (index >> bit) & 1
            spread = {}
            for g, part in parts.items():
                spread[g] = lax.dynamic_slice_in_dim(part, mine, 1, axis)
                spread[g | (1 << i)] = lax.dynamic_slice_in_dim(part, 1 - mine, 1, axis)
            parts = spread
        summed = parts[0].astype(wide)
        for g, part in parts.items():
            if g:
                mask = sum((1 << group[i]) for i in range(len(group)) if (g >> i) & 1)
                summed = summed + swap(part, axis_name, size, mask).astype(wide)
        return summed.astype(grad.dtype)

    for group in reversed(batch_rounds(bits)):
        held = halve(held, "batch", batch_size, b, group, zbits)
        if late is not None:
            late = halve(late, "batch", batch_size, b, group, zbits)
            held = jnp.concatenate([held, late], total + 1)
            late = None
    for bit in range(zbits):
        held = halve(held, "pos", pos_size, z, (bit,), 0)
    return held.reshape(rows, -1)


CHUNK = 512

lengths = (D, D, HID, GATE, GATE, SEQ, D)
ends = [sum(lengths[: i + 1]) for i in range(len(lengths))]
GAIN_IN, BIAS_IN, BIAS_HIDDEN, GAIN_GATE, BIAS_GATE, BIAS_SPATIAL, BIAS_OUT = (
    slice(end - n, end) for end, n in zip(ends, lengths)
)
VEC = ends[-1]


def shifted(outer, inner):
    return slice(outer.start + inner.start, outer.start + inner.stop)


tail_slope = 0.39 / math.sqrt(2.0)
tail_series = (
    0.23532609033994684,
    0.09138275083966492,
    0.6495739793206253,
    -0.6354188599562557,
    0.8866760936996321,
    -0.22754005589281026,
)
exp_scale = -0.5 / math.log(2.0)
density = 1.0 / math.sqrt(2.0 * math.pi)


def gelu_and_slope(v):
    size = jnp.abs(v)
    t = pl.reciprocal(1.0 + tail_slope * size)
    bell = jnp.exp2(exp_scale * (v * v))
    series = 0.5 * tail_series[-1]
    for c in reversed(tail_series[:-1]):
        series = series * t + 0.5 * c
    tail = series * t * bell
    phi = jnp.where(v > 0, 1.0 - tail, tail)
    return v * phi, phi + (density * v) * bell


def dot(a, b, ca=1, cb=0):
    return lax.dot_general(a, b, (((ca,), (cb,)), ((), ())), preferred_element_type=wide)


def column_blocks(k):
    return slice(k * CHUNK, (k + 1) * CHUNK)


def block_at(z, k, size, base=0):
    return pl.ds(pl.multiple_of(base + (z ^ k) * size, LANE), size)


def project_kernel(
    x_ref, w_ref, vec, scaled_ref, left_ref, slope_ref, normed_ref, inverse_ref, gate_ref, half_ref
):
    mine, _, length, _ = x_ref.shape
    total = mine * length
    normed, _ = norm_parts(x_ref[:, 0].reshape(total, D).astype(wide))
    scaled = (normed * vec[:, GAIN_IN] + vec[:, BIAS_IN]).astype(low_type)
    scaled_ref[:, 0] = scaled.reshape(mine, length, D)

    def part(step, base):
        at = pl.multiple_of(step * CHUNK, CHUNK)
        cols = pl.ds(pl.multiple_of(base + at, CHUNK), CHUNK)
        bias = vec[:, pl.ds(pl.multiple_of(BIAS_HIDDEN.start + base + at, CHUNK), CHUNK)]
        value, slope = gelu_and_slope(dot(scaled, w_ref[:, cols]) + bias)
        slope_ref[:, 0, :, cols] = slope.astype(low_type).reshape(mine, length, CHUNK)
        return pl.ds(at, CHUNK), value

    def body(step, carry):
        cols, value = part(step, 0)
        left_ref[:, 0, :, cols] = value.astype(low_type).reshape(mine, length, CHUNK)
        cols, value = part(step, GATE)
        half_ref[:, cols] = value
        return carry

    lax.fori_loop(0, GATE // CHUNK, body, 0, unroll=True)
    normed_gate, inverse = norm_parts(half_ref[...])
    inverse_ref[:, 0] = inverse.reshape(mine, length, 1)
    normed_ref[:, 0] = normed_gate.astype(low_type).reshape(mine, length, GATE)
    gate = (normed_gate * vec[:, GAIN_GATE] + vec[:, BIAS_GATE]).astype(low_type)
    gate_ref[:, 0] = gate.reshape(mine, length, GATE)


def mix_kernel(pos_size, *refs):
    (x_ref, seg_ref, pad_ref, skip_ref, ws_ref, wo_ref, vec, left_ref, gate_ref) = refs[:9]
    mixed_refs = refs[9 : 9 + pos_size]
    spatial_ref, gated_ref, mixing_ref, col_ref, line_ref = refs[9 + pos_size :]
    z = lax.axis_index("pos")
    row = z * pl.num_programs(0) + pl.program_id(0)
    length = x_ref.shape[1]
    part = length // pos_size
    places = range(pos_size)

    def line(ref):
        rows = jnp.concatenate([ref[:, block_at(z, k, part)] for k in places], 1)
        at = lax.broadcasted_iota(jnp.int32, rows.shape, 0)
        return jnp.sum(jnp.where(at == row, rows.astype(wide), 0.0), 0, keepdims=True)

    segment = line(seg_ref)
    padding = line(pad_ref)
    keep = padding * (1.0 - skip_ref[row].astype(wide))
    key = jnp.where(padding == 1.0, segment, -1.0)
    bias = jnp.concatenate([vec[:, block_at(z, k, part, BIAS_SPATIAL.start)] for k in places], 1)
    lines = jnp.concatenate([segment, keep, bias, key, jnp.zeros((4, length), wide)], 0)
    col = lines.T
    line_ref[0] = lines
    col_ref[0] = col
    weights = jnp.concatenate(
        [
            jnp.concatenate([ws_ref[block_at(z, i, part), block_at(z, j, part)] for j in places], 1)
            for i in places
        ],
        0,
    )
    masked = jnp.where(col[:, 0:1] == key, weights.astype(wide), 0.0)
    mixing = masked.astype(low_type)
    mixing_ref[0] = masked.T.astype(low_type)
    branch = jnp.zeros(x_ref.shape[1:], wide)
    for c in range(GATE // CHUNK):
        cols = column_blocks(c)
        spatial = dot(mixing, gate_ref[0, :, cols]) + col[:, 2:3]
        gated = (left_ref[0, :, cols].astype(wide) * spatial).astype(low_type)
        spatial_ref[0, :, cols] = spatial.astype(low_type)
        gated_ref[0, :, cols] = gated
        branch = branch + dot(gated, wo_ref[cols, :])
    mixed = (x_ref[0].astype(wide) + col[:, 1:2] * (branch + vec[:, BIAS_OUT])).astype(low_type)
    for k in places:
        mixed_refs[k][0] = mixed[k * part : (k + 1) * part]


def back_kernel(pos_size, *refs):
    cot_refs = refs[:pos_size]
    (
        col_ref, line_ref, mixing_ref, wo_ref, vec, left_ref, gate_ref, normed_ref, inverse_ref,
        spatial_ref, gated_ref, slope_ref, pre_ref, dwo_ref, dws_ref, dvec, dwo_acc, dws_acc, gate_acc,
    ) = refs[pos_size:]
    row = pl.program_id(0)
    z = lax.axis_index("pos")

    @pl.when(row == 0)
    def _():
        for ref in (dwo_acc, dws_acc, dvec):
            ref[...] = jnp.zeros_like(ref)

    col = col_ref[0]
    same = col[:, 0:1] == line_ref[0][3:4]
    mixing_back = mixing_ref[0]
    cot = jnp.concatenate([ref[0] for ref in cot_refs], 0)
    grad_branch = cot.astype(wide) * col[:, 1:2]
    dvec[:, BIAS_OUT] += jnp.sum(grad_branch, 0, keepdims=True)
    branch_low = grad_branch.astype(low_type)
    length = branch_low.shape[0]
    part = length // pos_size
    products = jnp.zeros((length, length), wide)
    first = jnp.zeros((length, 1), wide)
    cross = jnp.zeros((length, 1), wide)
    spatial_bias = jnp.zeros((8, length), wide)
    ones = jnp.ones((8, CHUNK), low_type)
    for c in range(GATE // CHUNK):
        cols = column_blocks(c)
        grad_gated = dot(branch_low, wo_ref[cols, :], 1, 1)
        dwo_acc[cols, :] += dot(gated_ref[0, :, cols], branch_low, 0, 0)
        spatial_low = (grad_gated * left_ref[0, :, cols].astype(wide)).astype(low_type)
        spatial_bias = spatial_bias + dot(ones, spatial_low, 1, 1)
        pre = (grad_gated * spatial_ref[0, :, cols].astype(wide)) * slope_ref[0, :, cols].astype(wide)
        pre_ref[0, :, cols] = pre.astype(low_type)
        dvec[:, shifted(BIAS_HIDDEN, cols)] += jnp.sum(pre, 0, keepdims=True)
        products = products + dot(spatial_low, gate_ref[0, :, cols], 1, 1)
        grad_gate = dot(mixing_back, spatial_low)
        normed = normed_ref[0, :, cols].astype(wide)
        dvec[:, shifted(GAIN_GATE, cols)] += jnp.sum(grad_gate * normed, 0, keepdims=True)
        dvec[:, shifted(BIAS_GATE, cols)] += jnp.sum(grad_gate, 0, keepdims=True)
        grad_hat = grad_gate * vec[:, shifted(GAIN_GATE, cols)]
        gate_acc[:, cols] = grad_hat
        first = first + jnp.sum(grad_hat, 1, keepdims=True)
        cross = cross + jnp.sum(grad_hat * normed, 1, keepdims=True)
    for k in range(pos_size):
        dvec[:, block_at(z, k, part, BIAS_SPATIAL.start)] += spatial_bias[0:1, k * part : (k + 1) * part]
    dws_acc[...] += jnp.where(same, products, 0.0)
    first = first * (1.0 / GATE)
    cross = cross * (1.0 / GATE)
    inverse = inverse_ref[0]
    for c in range(GATE // CHUNK):
        cols = column_blocks(c)
        rest = shifted(slice(GATE, HID), cols)
        normed = normed_ref[0, :, cols].astype(wide)
        grad_right = (gate_acc[:, cols] - first - normed * cross) * inverse
        pre = grad_right * slope_ref[0, :, rest].astype(wide)
        pre_ref[0, :, rest] = pre.astype(low_type)
        dvec[:, shifted(BIAS_HIDDEN, rest)] += jnp.sum(pre, 0, keepdims=True)

    @pl.when(row == pl.num_programs(0) - 1)
    def _():
        dwo_ref[...] = dwo_acc[...].astype(low_type)
        for i in range(pos_size):
            for j in range(pos_size):
                dws_ref[block_at(z, i, part), block_at(z, j, part)] = dws_acc[
                    i * part : (i + 1) * part, j * part : (j + 1) * part
                ].astype(low_type)


def input_kernel(pos_size, pre_ref, w_ref, x_ref, vec, dvec_in, *refs):
    pieces, dvec = refs[:pos_size], refs[pos_size]
    step = pl.program_id(0)
    mine, _, length, _ = x_ref.shape
    total = mine * length

    @pl.when(step == 0)
    def _():
        dvec[...] = dvec_in[...]

    normed, inverse = norm_parts(x_ref[:, 0].reshape(total, D).astype(wide))
    grad_scaled = dot(pre_ref[:, 0].reshape(total, HID), w_ref[...], 1, 1)
    dvec[:, GAIN_IN] += jnp.sum(grad_scaled * normed, 0, keepdims=True)
    dvec[:, BIAS_IN] += jnp.sum(grad_scaled, 0, keepdims=True)
    grad = norm_back(grad_scaled * vec[:, GAIN_IN], normed, inverse).astype(low_type)
    for k in range(pos_size):

        @pl.when(step == k)
        def _():
            pieces[k][...] = grad.reshape(mine, length, D)


def pack_kernel(rows, in_ref, vec_ref, ws_ref, wo_ref, block):
    def tiles(ref, first, count, start):
        for n in range(count):
            lines = ref[pl.ds(first + n, rows, stride=count), :]
            block[:, start + n * LANE : start + (n + 1) * LANE] = lines.astype(low_type)

    tiles(in_ref, 0, HID // LANE, 0)
    gap = jnp.zeros((rows - vec_ref.shape[0], LANE), wide)
    block[:, HID : HID + LANE] = jnp.concatenate([vec_ref[...], gap], 0).astype(low_type)
    tiles(ws_ref, 0, SEQ // LANE, HID + LANE)
    group = rows * (D // LANE)
    for g in range(wo_ref.shape[0] // group):
        tiles(wo_ref, g * group, D // LANE, HID + LANE + SEQ + g * D)


def pack(rows, *flats):
    lines = [flat.reshape(-1, LANE) for flat in flats]
    width = HID + LANE + SEQ + flats[3].shape[0] // rows
    return pl.pallas_call(
        functools.partial(pack_kernel, rows),
        out_shape=shaped(low_type, rows, width),
        cost_estimate=cost(0, 1 << 19),
        name="pack",
    )(*lines)


def project_halves_kernel(
    pos_size, rows, x_ref, own, other,
    scaled_ref, left_ref, slope_ref, normed_ref, inverse_ref, gate_ref, w_ref, ws_ref, wo_ref, vec_ref,
    half_ref, w_all,
):
    step = pl.program_id(0)
    core = lax.axis_index("batch") & 1
    half = pos_size * rows
    taps = wo_ref.shape[0] // (2 * half)
    lines = vec_ref.shape[1] // (2 * own.shape[0] * pos_size * LANE)

    def place(side, src):
        at = slice(side * half, (side + 1) * half)
        w_ref[at, :] = src[step, :, :HID]
        ws_ref[at, :] = src[step, :, HID + LANE : HID + LANE + SEQ]
        for z in range(pos_size):
            for g in range(taps):
                start = side * (taps * half) + (z * taps + g) * rows
                cols = slice(HID + LANE + SEQ + g * D, HID + LANE + SEQ + (g + 1) * D)
                wo_ref[start : start + rows, :] = src[step, z * rows : (z + 1) * rows, cols]

    def place_all(side, src):
        for q in range(src.shape[0]):
            w_all[(2 * q + side) * half : (2 * q + side + 1) * half, :] = src[q, :, :HID]
            for z in range(pos_size):
                for j in range(lines):
                    start = ((2 * q + side) * pos_size * lines + z * lines + j) * LANE
                    row = src[q, z * rows + j : z * rows + j + 1, HID : HID + LANE]
                    vec_ref[:, start : start + LANE] = row.astype(wide)

    for c in (0, 1):

        @pl.when((core == c) & (step == 0))
        def _():
            place_all(c, own)
            place_all(1 - c, other)

        @pl.when(core == c)
        def _():
            place(c, own)
            place(1 - c, other)

    project_kernel(
        x_ref, w_all, vec_ref, scaled_ref, left_ref, slope_ref, normed_ref, inverse_ref, gate_ref, half_ref
    )


def whole(*shape):
    return pl.BlockSpec(shape, lambda r: (0,) * len(shape))


def per_row(*shape):
    return pl.BlockSpec((1,) + shape, lambda r: (r,) + (0,) * len(shape))


def shaped(dtype, *shape):
    return jax.ShapeDtypeStruct(shape, dtype)


def cost(flops, size, rare=0):
    return pl.CostEstimate(flops=flops, transcendentals=rare, bytes_accessed=size)


def project(x, weights, rows=None):
    mine, pos_size, length, _ = x.shape
    block = lambda n: pl.BlockSpec((mine, 1, length, n), lambda i: (0, i, 0, 0))
    out = lambda dtype, n: shaped(dtype, mine, pos_size, length, n)
    part = lambda n, cols: pl.BlockSpec((n // pos_size, cols), lambda i: (i, 0))
    total = mine * pos_size * length
    out_specs = [block(D), block(GATE), block(HID), block(GATE), block(1), block(GATE)]
    out_shape = [
        out(low_type, D), out(low_type, GATE), out(low_type, HID),
        out(low_type, GATE), out(wide, 1), out(low_type, GATE),
    ]
    scratch = [pltpu.VMEM((mine * length, GATE), wide)]
    if rows is None:
        kernel = project_kernel
        in_specs = [block(D), whole(D, HID), whole(1, VEC)]
    else:
        kernel = functools.partial(project_halves_kernel, pos_size, rows)
        in_specs = [block(D)] + [whole(*half.shape) for half in weights]
        out_specs += [part(D, HID), part(SEQ, SEQ), part(GATE, D), whole(1, VEC)]
        out_shape += [
            shaped(low_type, D, HID), shaped(low_type, SEQ, SEQ), shaped(low_type, GATE, D), shaped(wide, 1, VEC),
        ]
        scratch += [pltpu.VMEM((D, HID), low_type)]
    return pl.pallas_call(
        kernel,
        grid=(pos_size,),
        in_specs=in_specs,
        out_specs=out_specs,
        out_shape=out_shape,
        scratch_shapes=scratch,
        cost_estimate=cost(2 * total * D * HID + 40 * total * HID, 20 << 20, 2 * total * HID),
        name="project",
    )(x, *weights)


def mix(pos_size, x, seg, pad, skip, ws, wo, vec, left, gate):
    mine, length, _ = x.shape
    part = length // pos_size
    return pl.pallas_call(
        functools.partial(mix_kernel, pos_size),
        grid=(mine,),
        in_specs=[
            per_row(length, D), whole(*seg.shape), whole(*pad.shape), pl.BlockSpec(memory_space=pltpu.SMEM),
            whole(length, length), whole(GATE, D), whole(1, VEC), per_row(length, GATE), per_row(length, GATE),
        ],
        out_specs=[per_row(part, D)] * pos_size
        + [
            per_row(length, GATE), per_row(length, GATE), per_row(length, length), per_row(length, 8),
            per_row(8, length),
        ],
        out_shape=[shaped(low_type, mine, part, D)] * pos_size
        + [
            shaped(low_type, mine, length, GATE),
            shaped(low_type, mine, length, GATE),
            shaped(low_type, mine, length, length),
            shaped(wide, mine, length, 8),
            shaped(wide, mine, 8, length),
        ],
        cost_estimate=cost(4 * mine * length * GATE * D, 16 << 20),
        name="mix",
    )(x, seg, pad, skip, ws, wo, vec, left, gate)


def back(pieces, col, line, mixing, wo, vec, left, gate, normed, inverse, spatial, gated, slope):
    pos_size = len(pieces)
    mine, part, _ = pieces[0].shape
    length = part * pos_size
    return pl.pallas_call(
        functools.partial(back_kernel, pos_size),
        grid=(mine,),
        in_specs=[per_row(part, D)] * pos_size
        + [
            per_row(length, 8), per_row(8, length), per_row(length, length), whole(GATE, D), whole(1, VEC),
            per_row(length, GATE), per_row(length, GATE), per_row(length, GATE), per_row(length, 1),
            per_row(length, GATE), per_row(length, GATE), per_row(length, HID),
        ],
        out_specs=[per_row(length, HID), whole(GATE, D), whole(length, length), whole(1, VEC)],
        out_shape=[
            shaped(low_type, mine, length, HID),
            shaped(low_type, GATE, D),
            shaped(low_type, length, length),
            shaped(wide, 1, VEC),
        ],
        scratch_shapes=[
            pltpu.VMEM((GATE, D), wide),
            pltpu.VMEM((length, length), wide),
            pltpu.VMEM((length, GATE), wide),
        ],
        cost_estimate=cost(8 * mine * length * GATE * D, 30 << 20),
        name="back",
    )(*pieces, col, line, mixing, wo, vec, left, gate, normed, inverse, spatial, gated, slope)


def input_back(pre, w, x, vec, dvec):
    mine, pos_size, length, _ = x.shape
    block = lambda n: pl.BlockSpec((mine, 1, length, n), lambda i: (0, i, 0, 0))
    return pl.pallas_call(
        functools.partial(input_kernel, pos_size),
        grid=(pos_size,),
        in_specs=[block(HID), whole(D, HID), block(D), whole(1, VEC), whole(1, VEC)],
        out_specs=[whole(mine, length, D)] * pos_size + [whole(1, VEC)],
        out_shape=[shaped(low_type, mine, length, D)] * pos_size + [shaped(wide, 1, VEC)],
        cost_estimate=cost(2 * mine * pos_size * length * D * HID, 12 << 20),
        name="input_back",
    )(pre, w, x, vec, dvec)


def local_fn(sizes):
    batch_size, pos_size = sizes

    def local(
        tokens,
        cotangent,
        segment_ids,
        pad_mask,
        skip_flags,
        in_master,
        spatial_master,
        out_master,
        vector_master,
        in_first,
        spatial_first,
        out_first,
        vector_first,
        in_second,
        spatial_second,
        out_second,
        vector_second,
    ):
        b = lax.axis_index("batch")
        z = lax.axis_index("pos")
        place = (b, z)
        devices = batch_size * pos_size
        rows = tokens.shape[0]
        length = tokens.shape[1]
        mine = rows // pos_size

        def exchange(parts):
            return [part if k == 0 else swap(part, "pos", pos_size, k) for k, part in enumerate(parts)]

        def split_rows(value):
            return [lax.dynamic_slice_in_dim(value, (z ^ k) * mine, mine, 0) for k in range(pos_size)]

        def join_rows(parts):
            for bit in range(bit_count(pos_size)):
                lower = ((z >> bit) & 1) == 0
                parts = [
                    jnp.where(
                        lower, jnp.concatenate([u, v], 0), jnp.concatenate([v, u], 0)
                    )
                    for u, v in zip(parts[0::2], parts[1::2])
                ]
            return parts[0]

        in_rows = D // devices
        in_width = HID
        spatial_rows = spatial_master.shape[0] // D
        vector_cols = vector_master.shape[0] // in_rows
        token_parts = exchange(split_rows(tokens))
        inputs = jnp.stack(token_parts, 1)
        back_parts = exchange(split_rows(cotangent))
        if in_rows % 16 == 0 and batch_size == 2 * pos_size:
            block = pack(in_rows, in_master, vector_master, spatial_master, out_master)
            halves = gather_blocks(block, sizes, place, halves=True)
            saved = project(inputs, halves, in_rows)
            weight_in, weight_spatial, weight_out, vec = saved[6:]
        else:
            in_block = in_master.astype(low_type).reshape(in_rows, -1)
            spatial_block = spatial_master.astype(low_type).reshape(-1, D)
            out_block = out_master.astype(low_type).reshape(-1, D)
            vector_block = vector_master.astype(low_type).reshape(in_rows, -1)
            vector_block = jnp.pad(vector_block, ((0, 0), (0, LANE - vector_cols)))
            in_all = gather_blocks(jnp.concatenate([in_block, vector_block], 1), sizes, place)
            rest_block = jnp.concatenate([spatial_block, out_block], 0)
            rest_all = gather_blocks(rest_block, sizes, place).reshape(devices, -1, D)
            weight_in = in_all[:, :in_width]
            vec = in_all[:, in_width : in_width + vector_cols].reshape(1, -1).astype(wide)
            weight_spatial = rest_all[:, :spatial_rows].reshape(SEQ, SEQ)
            weight_out = rest_all[:, spatial_rows:].reshape(GATE, D)
            saved = project(inputs, (weight_in, vec))
        by_row = lambda value: value.reshape(mine, SEQ, -1)
        inputs_low = by_row(inputs)
        scaled_in, left_half, slope, normed_gate, inverse_gate, gate_low = map(by_row, saved[:6])
        outs = mix(
            pos_size, inputs_low, segment_ids, pad_mask, skip_flags, weight_spatial, weight_out, vec,
            left_half, gate_low,
        )
        mixed_parts = exchange(outs[:pos_size])
        mixed = join_rows(mixed_parts)
        spatial, gated, mixing, col, line = outs[pos_size:]
        pre_low, grad_weight_out, grad_weight_spatial, grad_vector = back(
            back_parts, col, line, mixing, weight_out, vec, left_half, gate_low, normed_gate,
            inverse_gate, spatial, gated, slope,
        )
        scaled_in = scaled_in.reshape(-1, D)
        pre_low = pre_low.reshape(-1, HID)

        grad_rest = jnp.concatenate(
            [
                grad_weight_spatial.reshape(devices, spatial_rows, D),
                grad_weight_out.reshape(devices, -1, D),
            ],
            1,
        )
        rest_sum = reduce_blocks(grad_rest.reshape(-1, D), sizes, place)

        grad_weight_in = jnp.einsum("td,th->dh", scaled_in, pre_low, preferred_element_type=wide)
        grad_weight_in = grad_weight_in.astype(low_type)
        grad_weight_in, pre_low = lax.optimization_barrier((grad_weight_in, pre_low))
        outs = input_back(
            pre_low.reshape(mine, pos_size, length, HID), weight_in, inputs, vec, grad_vector
        )
        grad_parts = exchange(outs[:pos_size])
        input_grad = cotangent.astype(wide) + join_rows(grad_parts).astype(wide)
        grad_vector = outs[pos_size]

        vector_part = grad_vector.astype(low_type).reshape(in_rows * devices, -1)
        vector_part = jnp.pad(vector_part, ((0, 0), (0, LANE - vector_cols)))
        in_part = grad_weight_in.reshape(in_rows * devices, -1)
        in_sum = reduce_blocks(in_part, sizes, place, vector_part)

        shards = (
            in_sum[:, :in_width].reshape(-1).astype(wide),
            rest_sum[:spatial_rows].reshape(-1).astype(wide),
            rest_sum[spatial_rows:].reshape(-1).astype(wide),
            in_sum[:, in_width : in_width + vector_cols].reshape(-1).astype(wide),
        )
        in_new = adamw(in_master, in_first, in_second, shards[0], rate_in, decay_matrix)
        spatial_new = adamw(
            spatial_master, spatial_first, spatial_second, shards[1], rate_spatial, decay_matrix
        )
        out_new = adamw(out_master, out_first, out_second, shards[2], rate_out, decay_matrix)
        vector_new = adamw(vector_master, vector_first, vector_second, shards[3], rate_vector, 0.0)
        return (
            mixed,
            input_grad,
            in_new[0],
            in_new[1],
            in_new[2],
            spatial_new[0],
            spatial_new[1],
            spatial_new[2],
            out_new[0],
            out_new[1],
            out_new[2],
            vector_new[0],
            vector_new[1],
            vector_new[2],
        )

    return local


def solution(mesh):
    sizes = (mesh.shape["batch"], mesh.shape["pos"])
    flat = P(("batch", "pos"))
    acts = P("batch", "pos", None)
    placed = (acts, acts, P("batch", None), P("batch", None), P("batch")) + (flat,) * 12
    return jax.shard_map(
        local_fn(sizes),
        mesh=mesh,
        in_specs=placed,
        out_specs=(acts, acts) + (flat,) * 12,
        check_vma=False,
    )
```
